32 devices in a mesh: dp: 8 (over y, x, core), tensor: 4 (over z).
Axes of the slice: x: 2, y: 2, z: 4, core: 2. Of those that a mesh axis runs over, the one named last changes fastest.
Arguments:
- tokens: bfloat16 [16384, 1024], P(('dp', 'tensor')), may hold values from -6 to 6
- lengths: int32 [8], P('dp'), may hold values from 512 to 2048, as said below
- cotangent: bfloat16 [16384, 1024], P(('dp', 'tensor')), may hold values from -6 to 6
- attention_gain: float32 [1024], replicated, may hold values from 0.1 to 1.9
- attention_bias: float32 [1024], replicated, may hold values from -1 to 1
- query_weight: bfloat16 [1024, 1024], P('dp', 'tensor'), may hold values from -0.1875 to 0.1875
- key_weight: bfloat16 [1024, 1024], P('dp', 'tensor'), may hold values from -0.1875 to 0.1875
- value_weight: bfloat16 [1024, 1024], P('dp', 'tensor'), may hold values from -0.1875 to 0.1875
- out_weight: bfloat16 [1024, 1024], P('tensor', 'dp'), may hold values from -3 to 3
- feedforward_gain: float32 [1024], replicated, may hold values from 0.1 to 1.9
- feedforward_bias: float32 [1024], replicated, may hold values from -1 to 1
- gate_weight: bfloat16 [1024, 4096], P('dp', 'tensor'), may hold values from -0.1875 to 0.1875
- up_weight: bfloat16 [1024, 4096], P('dp', 'tensor'), may hold values from -0.1875 to 0.1875
- down_weight: bfloat16 [4096, 1024], P('tensor', 'dp'), may hold values from -0.09375 to 0.09375
Outputs:
- layer_out: bfloat16 [16384, 1024], P(('dp', 'tensor'))
- tokens_grad: bfloat16 [16384, 1024], P(('dp', 'tensor'))
- attention_gain_grad: float32 [1024], replicated
- attention_bias_grad: float32 [1024], replicated
- query_grad: float32 [1024, 1024], P('dp', 'tensor')
- key_grad: float32 [1024, 1024], P('dp', 'tensor')
- value_grad: float32 [1024, 1024], P('dp', 'tensor')
- out_grad: float32 [1024, 1024], P('tensor', 'dp')
- feedforward_gain_grad: float32 [1024], replicated
- feedforward_bias_grad: float32 [1024], replicated
- gate_grad: float32 [1024, 4096], P('dp', 'tensor')
- up_grad: float32 [1024, 4096], P('dp', 'tensor')
- down_grad: float32 [4096, 1024], P('tensor', 'dp')
The draws below stay inside these ranges and needn't reach their ends.
Inputs may be any that keep to these rules, and one draw needn't show every extreme that they name: `lengths`: real tokens of each window; its positions from that count on are padding and never serve as keys. Some window is full and some holds 512.
All inputs are finite; a program needn't handle non-finite values.
Results may differ from the reference program's by a relative error of at most 0.018.
Values may be sent and summed in bfloat16 or wider, within the bound.
No kernel may reach another device: no remote copies, remote signals or barrier semaphores. Data moves between devices by JAX's collectives and lax.ppermute only.
A program may use at most 192 MiB of HBM per device.

```python
import math
import jax
import jax.numpy as jnp
from jax import lax

D = 1024
HEADS = 16
HEAD = 64
FF = 4096
WIN = 2048
WINDOWS = 8
TOKENS = 16384


def draw_lengths(key, part):
    first_key = jax.random.fold_in(key, 11)
    second_key = jax.random.fold_in(key, 23)
    values = jax.random.randint(first_key, (WINDOWS,), WIN // 4, WIN + 1, dtype=jnp.int32)
    order = jax.random.permutation(second_key, WINDOWS)
    values = values.at[order[0]].set(WIN)
    values = values.at[order[1]].set(WIN // 4)
    return values.astype(jnp.int32)


def shard_levels(rng, dims, shards, least, high):
    gain = 1.0
    for position, blocks in shards:
        heights = jax.random.uniform(jax.random.fold_in(jax.random.fold_in(rng, 6), position), (blocks,), jnp.float32, least / len(shards), high / len(shards))
        gain = gain * jnp.repeat(jnp.exp(heights), dims[position] // blocks).reshape((-1,) + (1,) * (len(dims) - 1 - position))
    return gain


def noise(own_key, extent, spread, limit, shards=(), kind=jnp.bfloat16):
    level = shard_levels(own_key, extent, shards, -0.22, 0.18) if shards else 1.0
    result = jax.random.normal(own_key, extent, jnp.float32) * spread * level
    return jnp.minimum(jnp.maximum(result, -limit), limit).astype(kind)


def setup_inputs(seed: int = 0) -> dict:
    arg_keys = jax.random.split(jax.random.key(seed), 15)
    return {
        "tokens": noise(arg_keys[0], (TOKENS, D), 1.0, 6.0, ((0, 32),)),
        "lengths": draw_lengths(jax.random.fold_in(arg_keys[14], 71), 0),
        "cotangent": noise(arg_keys[2], (TOKENS, D), 1.0, 6.0, ((0, 32),)),
        "attention_gain": jnp.clip(1.0 + 0.18 * jax.random.normal(arg_keys[3], (D,), jnp.float32), 0.1, 1.9),
        "attention_bias": noise(arg_keys[4], (D,), 0.2, 1.0, (), jnp.float32),
        "query_weight": noise(arg_keys[5], (D, D), D ** -0.5, 0.1875, ((0, 8), (1, 4))),
        "key_weight": noise(arg_keys[6], (D, D), D ** -0.5, 0.1875, ((0, 8), (1, 4))),
        "value_weight": noise(arg_keys[7], (D, D), D ** -0.5, 0.1875, ((0, 8), (1, 4))),
        "out_weight": noise(arg_keys[8], (D, D), (max(D * 8 // WIN, 1)) ** -0.5, 3.0, ((0, 4), (1, 8))),
        "feedforward_gain": jnp.clip(1.0 + 0.18 * jax.random.normal(arg_keys[9], (D,), jnp.float32), 0.1, 1.9),
        "feedforward_bias": noise(arg_keys[10], (D,), 0.2, 1.0, (), jnp.float32),
        "gate_weight": noise(arg_keys[11], (D, FF), D ** -0.5, 0.1875, ((0, 8), (1, 4))),
        "up_weight": noise(arg_keys[12], (D, FF), D ** -0.5, 0.1875, ((0, 8), (1, 4))),
        "down_weight": noise(arg_keys[13], (FF, D), FF ** -0.5, 0.09375, ((0, 4), (1, 8))),
    }


@jax.custom_vjp
def low(v):
    return lax.optimization_barrier(v.astype(jnp.bfloat16)).astype(jnp.float32)

@jax.custom_vjp
def low_back(v):
    return v

def low_keep(v):
    return (low(v), None)

def low_pass(kept, grad):
    return (grad,)

def back_keep(v):
    return (v, None)

def back_low(kept, grad):
    return (low(grad),)
low.defvjp(low_keep, low_pass)
low_back.defvjp(back_keep, back_low)
EPSILON = 1e-05
MASKED = -1000000000.0
ROTARY_BASE = 10000.0

def dense(left, right):
    return jnp.dot(left, right, precision=lax.Precision.HIGHEST)

def normalize(inputs, scaling, offset):
    centered = inputs - lax.optimization_barrier(jnp.mean(inputs, axis=1, keepdims=True))
    inverse = lax.rsqrt(lax.optimization_barrier(jnp.mean(centered * centered, axis=1, keepdims=True)) + EPSILON)
    return centered * inverse * scaling + offset

def rotary_tables(row_total):
    positions = (jnp.arange(row_total, dtype=jnp.int32) % WIN).astype(jnp.float32)
    half_dim = HEAD // 2
    inverse = jnp.power(ROTARY_BASE, -jnp.arange(half_dim, dtype=jnp.int32).astype(jnp.float32) * 2.0 / HEAD)
    angles = positions[:, None] * inverse[None, :]
    angles = jnp.concatenate([angles, angles], axis=1)[:, None, :]
    return (jnp.cos(angles), jnp.sin(angles))

def rotate(values):
    half_dim = values.shape[-1] // 2
    return jnp.concatenate([-values[..., half_dim:], values[..., :half_dim]], axis=-1)

def rope(values, cosine, sine_table):
    return values * cosine + rotate(values) * sine_table

def window_layer(items, params, cosine, sine_table):
    inputs, key_valid = items
    attention_gain, attention_bias, query_weight, key_weight, value_weight, out_weight, feedforward_gain, feedforward_bias, gate_weight, up_weight, down_weight = params
    rows_first = low(normalize(inputs, attention_gain, attention_bias))
    query_raw = low_back(dense(rows_first, query_weight)).reshape(WIN, HEADS, HEAD)
    key_raw = low_back(dense(rows_first, key_weight)).reshape(WIN, HEADS, HEAD)
    value_rows = low(low_back(dense(rows_first, value_weight))).reshape(WIN, HEADS, HEAD)
    query_rot = low(rope(query_raw, cosine, sine_table))
    key_rot = low(rope(key_raw, cosine, sine_table))
    scores = jnp.einsum('qhd,khd->hqk', query_rot, key_rot, precision=lax.Precision.HIGHEST) * (1.0 / math.sqrt(HEAD))
    scores = low_back(scores)
    scores = jnp.where(key_valid[None, None, :], scores, MASKED)
    weights = low(jax.nn.softmax(scores, axis=-1))
    mixed = jnp.einsum('hqk,khd->qhd', weights, value_rows, precision=lax.Precision.HIGHEST).reshape(WIN, D)
    mixed = low(low_back(mixed))
    residual = inputs + low_back(dense(mixed, out_weight))
    rows_second = low(normalize(residual, feedforward_gain, feedforward_bias))
    gate_value = low_back(dense(rows_second, gate_weight))
    up_value = low_back(dense(rows_second, up_weight))
    hidden = low(jax.nn.silu(gate_value) * up_value)
    return residual + low_back(dense(hidden, down_weight))

def reference(tokens, lengths, cotangent, attention_gain, attention_bias, query_weight, key_weight, value_weight, out_weight, feedforward_gain, feedforward_bias, gate_weight, up_weight, down_weight):
    cosine, sine_table = rotary_tables(WIN)
    key_valid = jnp.arange(WIN, dtype=jnp.int32)[None, :] < lengths.astype(jnp.int32)[:, None]
    params = (attention_gain.astype(jnp.float32), attention_bias.astype(jnp.float32), query_weight.astype(jnp.float32), key_weight.astype(jnp.float32), value_weight.astype(jnp.float32), out_weight.astype(jnp.float32), feedforward_gain.astype(jnp.float32), feedforward_bias.astype(jnp.float32), gate_weight.astype(jnp.float32), up_weight.astype(jnp.float32), down_weight.astype(jnp.float32))
    inputs = tokens.astype(jnp.float32).reshape(WINDOWS, WIN, D)

    def whole(layer_inputs, layer_params):
        stepper = jax.checkpoint(lambda items: window_layer(items, layer_params, cosine, sine_table))
        return lax.map(stepper, (layer_inputs, key_valid))
    outputs, pull = jax.vjp(whole, inputs, params)
    grad_inputs, grad_params = pull(cotangent.astype(jnp.float32).reshape(WINDOWS, WIN, D))
    return (outputs.reshape(TOKENS, D).astype(jnp.bfloat16), grad_inputs.reshape(TOKENS, D).astype(jnp.bfloat16), grad_params[0], grad_params[1], grad_params[2], grad_params[3], grad_params[4], grad_params[5], grad_params[6], grad_params[7], grad_params[8], grad_params[9], grad_params[10])
```

```python
import functools
import math

import jax
import jax.numpy as jnp
from jax import lax
from jax.experimental import pallas as pl
from jax.experimental.pallas import tpu as pltpu
from jax.sharding import PartitionSpec as P

HEAD = 64
WIN = 2048
EPSILON = 1e-05
MASKED = -1000000000.0
ROTARY_BASE = 10000.0
SCALE = 1.0 / math.sqrt(HEAD)
SCORE_LOG2 = SCALE * math.log2(math.e)

BLOCK = 8
CORE = (1, 0)
SIDE = (2, 0)
FAR_SIDE = (4, 0)
NEAR = (0, 1)
FAR = (0, 2)

F32 = jnp.float32
BF16 = jnp.bfloat16
NT = (((1,), (1,)), ((), ()))
NN = (((1,), (0,)), ((), ()))
TN = (((0,), (0,)), ((), ()))
VMEM_BYTES = 56 * 1024 * 1024


def dot(left, right, dims):
    return lax.dot_general(left, right, dims, preferred_element_type=F32)


def pick(array, index, axis):
    return lax.dynamic_index_in_dim(array, index, axis, keepdims=False)


class Links:
    def __init__(self, mesh):
        self.nd = mesh.shape["dp"]
        self.nt = mesh.shape["tensor"]
        self.outer = self.nd // BLOCK
        self.groups = [[o * BLOCK + i for o in range(self.outer)] for i in range(BLOCK)]

    def move(self, array, rule):
        pairs = []
        for d in range(self.nd):
            for t in range(self.nt):
                target = rule(d, t)
                if target is not None:
                    pairs.append((d * self.nt + t, target[0] * self.nt + target[1]))
        return lax.ppermute(array, ("dp", "tensor"), pairs)

    def swap(self, array, mask):
        return self.move(array, lambda d, t: (d ^ mask[0], t ^ mask[1]))

    def up(self, array):
        return self.move(array, lambda d, t: (d, t + 1) if t < 3 else None)

    def down(self, array):
        return self.move(array, lambda d, t: (d, t - 1) if t > 0 else None)

    def total(self, array):
        for bit in range(self.nd.bit_length() - 1):
            array = array + self.swap(array, (1 << bit, 0))
        for bit in range(self.nt.bit_length() - 1):
            array = array + self.swap(array, (0, 1 << bit))
        return array

    def gather_outer(self, array, axis):
        if self.outer == 1:
            return array
        return lax.all_gather(array, "dp", axis=axis, tiled=True, axis_index_groups=self.groups)

    def scatter_outer(self, array, axis):
        if self.outer == 1:
            return array
        return lax.psum_scatter(
            array, "dp", scatter_dimension=axis, tiled=True, axis_index_groups=self.groups
        )


def normalize(inputs, scaling, offset):
    centered = inputs - jnp.mean(inputs, axis=1, keepdims=True)
    inverse = lax.rsqrt(jnp.mean(centered * centered, axis=1, keepdims=True) + EPSILON)
    unit_rows = centered * inverse
    return (unit_rows * scaling + offset, unit_rows, inverse)


def normalize_back(grad_rows, unit_rows, inverse, scaling):
    grad_unit = grad_rows * scaling
    centered = grad_unit - jnp.mean(grad_unit, axis=1, keepdims=True)
    grad_inputs = inverse * (
        centered - unit_rows * jnp.mean(grad_unit * unit_rows, axis=1, keepdims=True)
    )
    return (grad_inputs, jnp.sum(grad_rows * unit_rows, axis=0), jnp.sum(grad_rows, axis=0))


def cost(flops, moved, exps=0):
    return pl.CostEstimate(flops=int(flops), bytes_accessed=int(moved), transcendentals=int(exps))


def params():
    return pltpu.CompilerParams(vmem_limit_bytes=VMEM_BYTES)


def place_kernel(base_ref, *refs, parts):
    sources, target = refs[:-1], refs[-1]
    outer, _, rows, _ = target.shape
    step = pl.program_id(0)

    def write(source):
        width = source.shape[-1]
        for part in range(parts):
            block = source[0, part].reshape(outer, rows, width)
            target[:, 0, :, part * width : (part + 1) * width] = block

    per = BLOCK // len(sources)
    for index, source in enumerate(sources):
        pl.when(step // per == index)(functools.partial(write, source))


def place(sources, base, outer):
    _, parts, rows, width = sources[0].shape
    per = BLOCK // len(sources)
    out = pl.pallas_call(
        functools.partial(place_kernel, parts=parts),
        grid_spec=pltpu.PrefetchScalarGridSpec(
            num_scalar_prefetch=1,
            grid=(BLOCK,),
            in_specs=[
                pl.BlockSpec((1, parts, rows, width), lambda r, b: (r % per, 0, 0, 0))
                for _ in sources
            ],
            out_specs=pl.BlockSpec(
                (outer, 1, rows // outer, parts * width), lambda r, b: (0, r ^ b[0], 0, 0)
            ),
        ),
        out_shape=jax.ShapeDtypeStruct((outer, BLOCK, rows // outer, parts * width), BF16),
        compiler_params=params(),
        cost_estimate=cost(0, 4 * BLOCK * parts * rows * width),
        name="place",
    )(base, *sources)
    return out.reshape(BLOCK * rows, parts * width)


def place_hidden_kernel(base_ref, own, side, far, corner, inner_ref, down_ref):
    step = pl.program_id(0)
    outer, _, rows, _ = inner_ref.shape

    def write(first, second):
        for far_index, source in enumerate((first, second)):
            for near_index in range(2):
                column = (far_index * 2 + near_index) * 128
                for matrix in range(3):
                    block = source[near_index, 0, matrix].reshape(outer, rows, 128)
                    if matrix < 2:
                        at = matrix * 512 + column
                        inner_ref[:, 0, :, at : at + 128] = block
                    else:
                        down_ref[:, 0, :, column : column + 128] = block

    pl.when(step < 4)(functools.partial(write, own, far))
    pl.when(step >= 4)(functools.partial(write, side, corner))


def place_hidden(own, side, far, corner, base, outer):
    rows = own.shape[3]
    spec = pl.BlockSpec((2, 1, 3, rows, 128), lambda r, b: (0, r % 4, 0, 0, 0))
    inner, down = pl.pallas_call(
        place_hidden_kernel,
        grid_spec=pltpu.PrefetchScalarGridSpec(
            num_scalar_prefetch=1,
            grid=(BLOCK,),
            in_specs=[spec] * 4,
            out_specs=[
                pl.BlockSpec((outer, 1, rows // outer, 1024), lambda r, b: (0, r ^ b[0], 0, 0)),
                pl.BlockSpec((outer, 1, rows // outer, 512), lambda r, b: (0, r ^ b[0], 0, 0)),
            ],
        ),
        out_shape=[
            jax.ShapeDtypeStruct((outer, BLOCK, rows // outer, 1024), BF16),
            jax.ShapeDtypeStruct((outer, BLOCK, rows // outer, 512), BF16),
        ],
        compiler_params=params(),
        cost_estimate=cost(0, 4 * BLOCK * rows * 1536),
        name="place_hidden",
    )(base, own, side, far, corner)
    return inner.reshape(BLOCK * rows, 1024), down.reshape(BLOCK * rows, 512)


def deliver_kernel(base_ref, source, gate_ref, up_ref, down_ref):
    gate_ref[...] = source[0, 0].astype(F32)
    up_ref[...] = source[0, 1].astype(F32)
    down_ref[...] = source[0, 2].astype(F32).T


def deliver(source, base):
    rows = source.shape[2]
    wide = pl.BlockSpec((rows, 128), lambda k, b: (0, k ^ b[0]))
    return pl.pallas_call(
        deliver_kernel,
        grid_spec=pltpu.PrefetchScalarGridSpec(
            num_scalar_prefetch=1,
            grid=(BLOCK,),
            in_specs=[pl.BlockSpec((1, 3, rows, 128), lambda k, b: (k, 0, 0, 0))],
            out_specs=[wide, wide, pl.BlockSpec((128, rows), lambda k, b: (k ^ b[0], 0))],
        ),
        out_shape=[
            jax.ShapeDtypeStruct((rows, 1024), F32),
            jax.ShapeDtypeStruct((rows, 1024), F32),
            jax.ShapeDtypeStruct((1024, rows), F32),
        ],
        compiler_params=params(),
        cost_estimate=cost(0, 6 * source.size),
        name="deliver",
    )(base, source)


def turned(values, lane):
    return jnp.where(lane % HEAD < HEAD // 2, pltpu.roll(values, 96, 1), pltpu.roll(values, 32, 1))


def project_kernel(
    order_ref, rows_ref, weight_ref, cos_ref, sin_ref, q_ref, k_ref, v_ref, kt_ref, vt_ref, h_ref
):
    rows = rows_ref[...]
    h_ref[...] = rows
    raw = dot(rows, weight_ref[...], NN)
    cosine, sine = cos_ref[...], sin_ref[...]
    lane = lax.broadcasted_iota(jnp.int32, cosine.shape, 1)
    width = q_ref.shape[1]
    for target, first in ((q_ref, 0), (k_ref, width)):
        for column in range(0, width, 128):
            tile = raw[:, first + column : first + column + 128]
            target[:, column : column + 128] = (tile * cosine + turned(tile, lane) * sine).astype(
                BF16
            )
    values = raw[:, 2 * width :]
    v_ref[...] = values.astype(BF16)
    vt_ref[...] = values.T.astype(BF16)
    kt_ref[...] = k_ref[...].astype(F32).T.astype(BF16)


def project(rows, weight, cosine, sine, order, width, step=256):
    depth = rows.shape[1]
    narrow = pl.BlockSpec((step, width), lambda j, o: (o[j], 0))
    tall = pl.BlockSpec((width, step), lambda j, o: (0, o[j]))
    table = pl.BlockSpec((step, 128), lambda j, o: (o[j], 0))
    flat = jax.ShapeDtypeStruct((WIN, width), BF16)
    deep = jax.ShapeDtypeStruct((width, WIN), BF16)
    return pl.pallas_call(
        project_kernel,
        grid_spec=pltpu.PrefetchScalarGridSpec(
            num_scalar_prefetch=1,
            grid=(WIN // step,),
            in_specs=[
                pl.BlockSpec((step, depth), lambda j, o: (j, 0)),
                pl.BlockSpec((depth, 3 * width), lambda j, o: (0, 0)),
                table,
                table,
            ],
            out_specs=[
                narrow,
                narrow,
                narrow,
                tall,
                tall,
                pl.BlockSpec((step, depth), lambda j, o: (o[j], 0)),
            ],
        ),
        out_shape=[flat, flat, flat, deep, deep, jax.ShapeDtypeStruct((WIN, depth), BF16)],
        compiler_params=params(),
        cost_estimate=cost(6 * WIN * depth * width, 6 * WIN * depth),
        name="project",
    )(order, rows, weight, cosine, sine)


def attend_kernel(q_ref, k_ref, vt_ref, bias_ref, o_ref, lse_ref, *, step):
    rows = q_ref.shape[0]
    lane = lax.broadcasted_iota(jnp.int32, (rows, 128), 1)
    query = q_ref[...]
    mixed = []
    for head in range(2):
        own = (lane >= HEAD) == (head == 1)
        masked_query = jnp.where(own, query, jnp.zeros_like(query))
        place_v = slice(HEAD * head, HEAD * head + HEAD)
        top = None
        for first in range(0, WIN, step):
            keys = slice(first, first + step)
            scores = dot(k_ref[keys, :], masked_query, NT) * SCORE_LOG2 + bias_ref[keys, :1]
            block_top = jnp.max(scores, axis=0, keepdims=True)
            new_top = block_top if top is None else jnp.maximum(top, block_top)
            weights = jnp.exp2(scores - new_top)
            part = dot(vt_ref[place_v, keys], weights.astype(BF16), NN)
            part_sum = jnp.sum(weights, axis=0, keepdims=True)
            if top is None:
                sums, total = part, part_sum
            else:
                fade = jnp.exp2(top - new_top)
                sums, total = sums * fade + part, total * fade + part_sum
            top = new_top
        mixed.append(sums * (1.0 / total))
        lse_ref[0, head : head + 1, :] = top + jnp.log2(total)
    o_ref[...] = jnp.concatenate(mixed, axis=0).T.astype(BF16)


def attend(query, key, value_t, bias, rows=1024, step=512):
    width = query.shape[1]
    pairs = width // 128
    return pl.pallas_call(
        functools.partial(attend_kernel, step=step),
        grid=(pairs, WIN // rows),
        in_specs=[
            pl.BlockSpec((rows, 128), lambda p, i: (i, p)),
            pl.BlockSpec((WIN, 128), lambda p, i: (0, p)),
            pl.BlockSpec((128, WIN), lambda p, i: (p, 0)),
            pl.BlockSpec((WIN, 128), lambda p, i: (0, 0)),
        ],
        out_specs=[
            pl.BlockSpec((rows, 128), lambda p, i: (i, p)),
            pl.BlockSpec((1, 2, rows), lambda p, i: (p, 0, i)),
        ],
        out_shape=[
            jax.ShapeDtypeStruct((WIN, width), BF16),
            jax.ShapeDtypeStruct((pairs, 2, WIN), F32),
        ],
        compiler_params=params(),
        cost_estimate=cost(16 * WIN * WIN * width, 8 * WIN * width, WIN * WIN * width // HEAD),
        name="attend",
    )(query, key, value_t, bias)


def attend_back_kernel(
    q_ref, k_ref, v_ref, kt_ref, o_ref, do_ref, lse_ref, bias_ref, cosq_ref, sinq_ref, cos_ref,
    sin_ref, dq_ref, dk_ref, dv_ref, dk_sum, dv_sum, *, step,
):
    rows = q_ref.shape[0]
    index = pl.program_id(1)

    @pl.when(index == 0)
    def _():
        dk_sum[...] = jnp.zeros_like(dk_sum)
        dv_sum[...] = jnp.zeros_like(dv_sum)

    lane = lax.broadcasted_iota(jnp.int32, (rows, 128), 1)
    query, grad = q_ref[...], do_ref[...]
    product = (grad.astype(F32) * o_ref[...].astype(F32)).T
    grad_query = []
    for head in range(2):
        own = (lane >= HEAD) == (head == 1)
        masked_query = jnp.where(own, query, jnp.zeros_like(query))
        masked_grad = jnp.where(own, grad, jnp.zeros_like(grad))
        part = slice(HEAD * head, HEAD * head + HEAD)
        row_dot = jnp.sum(product[part, :], axis=0, keepdims=True)
        log_total = lse_ref[0, head : head + 1, :]
        sums = None
        for first in range(0, WIN, step):
            keys = slice(first, first + step)
            scores = dot(k_ref[keys, :], masked_query, NT) * SCORE_LOG2 + bias_ref[keys, :1]
            weights = jnp.exp2(scores - log_total)
            grad_weights = dot(v_ref[keys, :], masked_grad, NT)
            grad_scores = (weights * (grad_weights - row_dot)).astype(BF16)
            dv_sum[keys, :] += dot(weights.astype(BF16), masked_grad, NN)
            dk_sum[keys, :] += dot(grad_scores, masked_query, NN)
            more = dot(kt_ref[part, keys], grad_scores, NN)
            sums = more if sums is None else sums + more
        grad_query.append(sums)

    def unturn(values, cosine, sine):
        at = lax.broadcasted_iota(jnp.int32, values.shape, 1)
        return ((values * cosine - turned(values, at) * sine) * SCALE).astype(BF16)

    dq_ref[...] = unturn(jnp.concatenate(grad_query, axis=0).T, cosq_ref[...], sinq_ref[...])

    @pl.when(index == pl.num_programs(1) - 1)
    def _():
        dk_ref[...] = unturn(dk_sum[...], cos_ref[...], sin_ref[...])
        dv_ref[...] = dv_sum[...].astype(BF16)


def attend_back(query, key, value, key_t, mixed, grad, lse, bias, cosine, sine, rows=512, step=512):
    width = query.shape[1]
    pairs = width // 128
    block = pl.BlockSpec((rows, 128), lambda p, i: (i, p))
    whole = pl.BlockSpec((WIN, 128), lambda p, i: (0, p))
    fixed = pl.BlockSpec((WIN, 128), lambda p, i: (0, 0))
    local = pl.BlockSpec((rows, 128), lambda p, i: (i, 0))
    return pl.pallas_call(
        functools.partial(attend_back_kernel, step=step),
        grid=(pairs, WIN // rows),
        in_specs=[
            block,
            whole,
            whole,
            pl.BlockSpec((128, WIN), lambda p, i: (p, 0)),
            block,
            block,
            pl.BlockSpec((1, 2, rows), lambda p, i: (p, 0, i)),
            fixed,
            local,
            local,
            fixed,
            fixed,
        ],
        out_specs=[block, whole, whole],
        out_shape=[jax.ShapeDtypeStruct((WIN, width), BF16)] * 3,
        scratch_shapes=[pltpu.VMEM((WIN, 128), F32)] * 2,
        compiler_params=params(),
        cost_estimate=cost(40 * WIN * WIN * width, 16 * WIN * width, WIN * WIN * width // HEAD),
        name="attend_back",
    )(query, key, value, key_t, mixed, grad, lse, bias, cosine, sine, cosine, sine)


def unproject_kernel(order_ref, dq_ref, dk_ref, dv_ref, weight_ref, out_ref):
    width = dq_ref.shape[1]
    total = dot(dq_ref[...], weight_ref[:, :width], NT)
    total += dot(dk_ref[...], weight_ref[:, width : 2 * width], NT)
    total += dot(dv_ref[...], weight_ref[:, 2 * width :], NT)
    out_ref[...] = total.astype(BF16)


def unproject(grads, weight, order, step=256):
    depth, triple = weight.shape
    width = triple // 3
    spec = pl.BlockSpec((step, width), lambda j, o: (o[j], 0))
    return pl.pallas_call(
        unproject_kernel,
        grid_spec=pltpu.PrefetchScalarGridSpec(
            num_scalar_prefetch=1,
            grid=(WIN // step,),
            in_specs=[spec, spec, spec, pl.BlockSpec((depth, triple), lambda j, o: (0, 0))],
            out_specs=pl.BlockSpec((step, depth), lambda j, o: (j, 0)),
        ),
        out_shape=jax.ShapeDtypeStruct((WIN, depth), BF16),
        compiler_params=params(),
        cost_estimate=cost(2 * WIN * depth * triple, 4 * WIN * depth),
        name="unproject",
    )(order, *grads, weight)


def add(*arrays):
    total = arrays[0].astype(F32)
    for array in arrays[1:]:
        total = total + array.astype(F32)
    return total.astype(BF16)


def collect_window(links, rows, core, line):
    half = rows.shape[0] // 2
    keep = lax.dynamic_slice_in_dim(rows, core * half, half, 0)
    give = lax.dynamic_slice_in_dim(rows, (1 - core) * half, half, 0)
    other = links.swap(give, CORE)
    first = jnp.where(core == 0, keep, other)
    second = jnp.where(core == 0, other, keep)
    low = line < 2
    down1, up1 = links.down(first), links.up(second)
    down2 = links.down(jnp.where(line == 3, second, down1))
    up2 = links.up(jnp.where(line == 0, first, up1))
    last = links.move(
        jnp.where(line == 1, down2, up2),
        lambda d, t: {1: (d, 0), 2: (d, 3)}.get(t),
    )
    slots = (
        jnp.where(low, first, second),
        jnp.where(low, down1, up1),
        jnp.where(low, down2, up2),
        jnp.where((line == 0) | (line == 3), last, jnp.where(line == 1, up2, down2)),
    )
    pieces = []
    for slot in slots:
        pieces += [slot, links.swap(slot, CORE)]
    return jnp.concatenate(pieces, axis=0)


def return_window(links, parts, core, line):
    mine = add(parts[0], links.swap(parts[1], CORE))
    zero = jnp.zeros_like(mine[0])
    low = line < 2
    last = links.move(mine[3], lambda d, t: {0: (d, 1), 3: (d, 2)}.get(t))
    third = add(mine[2], last)
    up2 = links.up(jnp.where(low, third, mine[3]))
    down2 = links.down(jnp.where(low, mine[3], third))
    up1 = links.up(add(jnp.where(low, mine[1], zero), up2))
    down1 = links.down(add(jnp.where(low, zero, mine[1]), down2))
    first = add(jnp.where(low, mine[0], zero), up1, jnp.where(line == 0, down2, zero))
    second = add(jnp.where(low, zero, mine[0]), down1, jnp.where(line == 3, up2, zero))
    keep = jnp.where(core == 0, first, second)
    other = links.swap(jnp.where(core == 0, second, first), CORE)
    return jnp.where(
        core == 0,
        jnp.concatenate([keep, other], axis=0),
        jnp.concatenate([other, keep], axis=0),
    )


def collect_block(links, rows):
    half = rows.shape[0] // 2
    side, near = links.swap(rows, SIDE), links.swap(rows, NEAR)
    corner = [links.swap(near[:half], SIDE), links.swap(side[half:], NEAR)]
    chunks = [[rows], [side], [near], corner]
    return [
        jnp.concatenate(chunk + [links.swap(part, CORE) for part in chunk], axis=0)
        for chunk in chunks
    ]


def return_block(links, parts):
    rows = parts[0].shape[0] // 2
    half = rows // 2
    own, side, near, corner = (add(part[:rows], links.swap(part[rows:], CORE)) for part in parts)
    to_near = links.swap(corner[:half], SIDE)
    to_side = links.swap(corner[half:], NEAR)
    near = jnp.concatenate([add(near[:half], to_near), near[half:]], axis=0)
    side = jnp.concatenate([side[:half], add(side[half:], to_side)], axis=0)
    return (
        own.astype(F32)
        + links.swap(side, SIDE).astype(F32)
        + links.swap(near, NEAR).astype(F32)
    )


def per_device(
    links,
    tokens,
    lengths,
    cotangent,
    attention_gain,
    attention_bias,
    query_weight,
    key_weight,
    value_weight,
    out_weight,
    feedforward_gain,
    feedforward_bias,
    gate_weight,
    up_weight,
    down_weight,
):
    outer = links.outer
    dp = lax.axis_index("dp")
    line = lax.axis_index("tensor")
    core, inner = dp % 2, dp % BLOCK
    side_bit, far_bit = dp // 2 % 2, dp // 4 % 2
    near_bit = line % 2
    window = line // 2
    share = near_bit * 2 + core
    width = query_weight.shape[1]
    depth = tokens.shape[1]
    chunk = tokens.shape[0]

    def scalar(value):
        return jnp.reshape(value, (1,)).astype(jnp.int32)

    inputs = tokens.astype(F32)
    normed_first, unit_first, inverse_first = normalize(inputs, attention_gain, attention_bias)
    arrived = collect_window(links, normed_first.astype(BF16), core, line)

    qkv = links.gather_outer(jnp.stack([query_weight, key_weight, value_weight]), 1)
    pair = jnp.stack(
        [
            links.move(
                qkv, lambda d, t, k=k: ((d & ~1) | (t % 2), t // 2 + 2 * ((d & 1) ^ k))
            )
            for k in range(2)
        ]
    )
    quad = jnp.concatenate([pair, links.swap(pair, SIDE)], axis=0)
    attention_base = (inner // 2) * 2 + window
    weight_qkv = place([quad, links.swap(quad, FAR_SIDE)], scalar(attention_base), outer)

    piece = links.gather_outer(out_weight.T, 0)[None]
    piece = jnp.concatenate([piece, links.swap(piece, NEAR)], axis=0)
    piece = jnp.concatenate([piece, links.swap(piece, FAR)], axis=0)[None]
    piece = jnp.concatenate([piece, links.swap(piece, SIDE)], axis=0)
    piece = jnp.concatenate([piece, links.swap(piece, FAR_SIDE)], axis=0)
    both = jnp.stack([piece, links.swap(piece, CORE)], axis=1)
    weight_out = place([both.reshape((BLOCK,) + both.shape[2:])], scalar(inner), outer)

    packed = links.gather_outer(jnp.stack([gate_weight, up_weight, down_weight.T]), 1)
    rows_each = packed.shape[1]
    packed = packed.reshape(3, rows_each, 2, 2, 2, 128).transpose(2, 3, 4, 0, 1, 5)

    def trade(array, bit, axis, mask):
        kept, given = pick(array, bit, axis), pick(array, 1 - bit, axis)
        return kept, links.swap(given, mask)

    kept, got = trade(packed, core, 2, CORE)
    packed = jnp.stack([kept, got])
    kept, got = trade(packed, side_bit, 2, SIDE)
    packed = jnp.stack([kept, got])
    kept, got = trade(packed, near_bit, 2, NEAR)
    packed = jnp.stack([kept, got]).reshape(2, 4, 3, rows_each, 128)
    far = links.swap(packed, FAR)
    weight_in, weight_down = place_hidden(
        packed,
        links.swap(packed, FAR_SIDE),
        far,
        links.swap(far, FAR_SIDE),
        scalar(inner),
        outer,
    )

    cot_chunks = collect_block(links, cotangent)

    order_chunk = jnp.arange(4, dtype=jnp.int32) ^ share
    positions = (order_chunk[:, None] * chunk + jnp.arange(chunk, dtype=jnp.int32)).reshape(-1)
    lane = jnp.arange(128, dtype=jnp.int32)
    frequency = jnp.power(ROTARY_BASE, -(lane % (HEAD // 2)).astype(F32) * 2.0 / HEAD)
    angles = positions.astype(F32)[:, None] * frequency[None, :]
    cosine = jnp.cos(angles)
    sine = jnp.sin(angles) * jnp.where(lane % HEAD < HEAD // 2, -1.0, 1.0)
    length = jnp.where(core == window, lengths, links.swap(lengths, CORE))
    bias = jnp.where(positions < length[0], 0.0, MASKED).astype(F32)
    bias = jnp.broadcast_to(bias[:, None], (WIN, 128))

    slot = jnp.arange(4, dtype=jnp.int32)
    slot_chunk = jnp.where(line < 2, line + slot, line - slot) % 4
    slot_place = (slot_chunk ^ share) * 2
    order_in = (slot_place[:, None] + jnp.stack([core, 1 - core])[None, :]).reshape(-1)
    order_out = (slot_place[None, :] + jnp.stack([core, 1 - core])[:, None]).reshape(-1)
    query, key, value, key_t, value_t, rows_first = project(
        arrived, weight_qkv, cosine, sine, order_in.astype(jnp.int32), width
    )
    mixed, lse = attend(query, key, value_t, bias)

    def to_owner(k):
        def rule(d, t):
            return (d & ~1) | (t // 2), ((t % 2) * 2 + (d & 1)) ^ k

        return rule

    def to_heads(k):
        def rule(d, t):
            who = t ^ k
            return (d & ~1) | (who & 1), (who >> 1) + 2 * (d & 1)

        return rule

    attended = jnp.concatenate(
        [links.move(mixed[k * chunk : (k + 1) * chunk], to_owner(k)) for k in range(4)], axis=1
    )
    residual = inputs + dot(attended, weight_out, NT)
    normed_second, unit_second, inverse_second = normalize(
        residual, feedforward_gain, feedforward_bias
    )
    row_chunks = collect_block(links, normed_second.astype(BF16))

    hidden_width = weight_down.shape[1]
    down_parts, back_parts = [], []
    grad_in, grad_down = 0.0, 0.0
    for rows, cot in zip(row_chunks, cot_chunks, strict=True):
        gate_up = dot(rows, weight_in, NN)
        gate, up = gate_up[:, :hidden_width], gate_up[:, hidden_width:]
        sigmoid = jax.nn.sigmoid(gate)
        activated = gate * sigmoid
        hidden = (activated * up).astype(BF16)
        grad_hidden = dot(cot, weight_down, NN)
        grad_gate = grad_hidden * up * sigmoid * (1.0 + gate * (1.0 - sigmoid))
        grad_both = jnp.concatenate([grad_gate, grad_hidden * activated], axis=1).astype(BF16)
        down_parts.append(dot(hidden, weight_down, NT).astype(BF16))
        back_parts.append(dot(grad_both, weight_in, NT).astype(BF16))
        grad_in = grad_in + dot(rows, grad_both, TN)
        grad_down = grad_down + dot(cot, hidden, TN)

    grad_normed_second = return_block(links, back_parts)
    layer_out = (residual + return_block(links, down_parts)).astype(BF16)
    grad_mid, gain_second, bias_second = normalize_back(
        grad_normed_second, unit_second, inverse_second, feedforward_gain
    )
    grad_residual = cotangent.astype(F32) + grad_mid
    grad_attn = grad_residual.astype(BF16)
    grad_attended = dot(grad_attn, weight_out, NN).astype(BF16)
    grad_mixed = jnp.concatenate(
        [
            links.move(grad_attended[:, k * width : (k + 1) * width], to_heads(k))
            for k in range(4)
        ],
        axis=0,
    )
    grad_out = dot(grad_attn, attended, TN).astype(BF16)

    grads = attend_back(query, key, value, key_t, mixed, grad_mixed, lse, bias, cosine, sine)
    parts = unproject(grads, weight_qkv, order_out.astype(jnp.int32))
    grad_normed_first = return_window(
        links, parts.reshape(2, 4, chunk // 2, depth), core, line
    ).astype(F32)
    grad_low, gain_first, bias_first = normalize_back(
        grad_normed_first, unit_first, inverse_first, attention_gain
    )
    tokens_grad = (grad_residual + grad_low).astype(BF16)
    norm_second = links.total(jnp.stack([gain_second, bias_second]))
    norm_first = links.total(jnp.stack([gain_first, bias_first]))

    sums = jnp.concatenate([grad_in, grad_down], axis=1).astype(BF16)
    sums = sums.reshape(outer, 2, 2, 2, depth // (outer * BLOCK), 3, 2, 2, 128)
    kept, got = trade(sums, far_bit, 1, FAR_SIDE)
    sums = add(kept, got)
    sums = add(sums[..., 0, :, :], links.swap(sums[..., 1, :, :], FAR))
    sums = jnp.stack([sums[..., 0, :], links.swap(sums[..., 1, :], NEAR)])
    kept, got = trade(sums, side_bit, 2, SIDE)
    sums = jnp.stack([kept, got], axis=1)
    kept, got = trade(sums, core, 3, CORE)
    sums = jnp.stack([kept, got], axis=2)
    sums = sums.transpose(0, 1, 2, 5, 3, 4, 6).reshape(BLOCK, 3, rows_each, 128)
    sums = links.scatter_outer(sums, 2)
    gate_grad, up_grad, down_grad = deliver(sums, scalar(near_bit * 4 + side_bit * 2 + core))

    sums = grad_out.reshape(outer, 2, 2, 2, depth // (outer * BLOCK), 2, 2, width)
    sums = add(*trade(sums, core, 3, CORE))
    sums = add(*trade(sums, far_bit, 1, FAR_SIDE))
    sums = add(*trade(sums, side_bit, 1, SIDE))
    sums = add(sums[:, :, 0], links.swap(sums[:, :, 1], FAR))
    sums = add(sums[:, :, 0], links.swap(sums[:, :, 1], NEAR))
    sums = links.scatter_outer(sums.reshape(rows_each, width), 0)
    out_grad = sums.astype(F32).T

    sums = jnp.concatenate([dot(rows_first, grad, TN) for grad in grads], axis=1).astype(BF16)
    sums = sums.reshape(outer, 2, 2, 2, depth // (outer * BLOCK), 3 * width)
    sums = add(*trade(sums, far_bit, 1, FAR_SIDE))
    sums = add(*trade(sums, side_bit, 1, SIDE))
    halves = []
    for k in range(2):
        piece = pick(sums, window ^ k, 1)
        halves.append(
            links.move(
                piece, lambda d, t, k=k: ((d & ~1) | ((t // 2) ^ k), (t % 2) * 2 + (d & 1))
            )
        )
    sums = links.scatter_outer(add(*halves).reshape(rows_each, 3 * width), 0).astype(F32)
    return (
        layer_out,
        tokens_grad,
        norm_first[0],
        norm_first[1],
        sums[:, :width],
        sums[:, width : 2 * width],
        sums[:, 2 * width :],
        out_grad,
        norm_second[0],
        norm_second[1],
        gate_grad,
        up_grad,
        down_grad,
    )


def solution(mesh):
    rows, columns = P("dp", "tensor"), P("tensor", "dp")
    spread = P(("dp", "tensor"), None)
    placed = (
        spread, P("dp"), spread, P(), P(), rows, rows, rows, columns, P(), P(), rows, rows, columns
    )
    given = (
        spread, spread, P(), P(), rows, rows, rows, columns, P(), P(), rows, rows, columns
    )
    return jax.shard_map(
        functools.partial(per_device, Links(mesh)),
        mesh=mesh,
        in_specs=placed,
        out_specs=given,
        check_vma=False,
    )
```

```python
import functools
import math

import jax
import jax.numpy as jnp
from jax import lax
from jax.experimental import pallas as pl
from jax.experimental.pallas import tpu as pltpu
from jax.sharding import PartitionSpec as P

HEAD = 64
WIN = 2048
EPSILON = 1e-05
MASKED = -1000000000.0
ROTARY_BASE = 10000.0
SCALE = 1.0 / math.sqrt(HEAD)
SCORE_LOG2 = SCALE * math.log2(math.e)

BLOCK = 8
CORE = (1, 0)
SIDE = (2, 0)
FAR_SIDE = (4, 0)
NEAR = (0, 1)
FAR = (0, 2)

F32 = jnp.float32
BF16 = jnp.bfloat16
NT = (((1,), (1,)), ((), ()))
NN = (((1,), (0,)), ((), ()))
TN = (((0,), (0,)), ((), ()))
VMEM_BYTES = 56 * 1024 * 1024


def dot(left, right, dims):
    return lax.dot_general(left, right, dims, preferred_element_type=F32)


def pick(array, index, axis):
    return lax.dynamic_index_in_dim(array, index, axis, keepdims=False)


class Links:
    def __init__(self, mesh):
        self.nd = mesh.shape["dp"]
        self.nt = mesh.shape["tensor"]
        self.outer = self.nd // BLOCK
        self.groups = [[o * BLOCK + i for o in range(self.outer)] for i in range(BLOCK)]

    def move(self, array, rule):
        pairs = []
        for d in range(self.nd):
            for t in range(self.nt):
                target = rule(d, t)
                if target is not None:
                    pairs.append((d * self.nt + t, target[0] * self.nt + target[1]))
        return lax.ppermute(array, ("dp", "tensor"), pairs)

    def swap(self, array, mask):
        return self.move(array, lambda d, t: (d ^ mask[0], t ^ mask[1]))

    def up(self, array):
        return self.move(array, lambda d, t: (d, t + 1) if t < 3 else None)

    def down(self, array):
        return self.move(array, lambda d, t: (d, t - 1) if t > 0 else None)

    def gather_outer(self, array, axis):
        if self.outer == 1:
            return array
        return lax.all_gather(array, "dp", axis=axis, tiled=True, axis_index_groups=self.groups)

    def scatter_outer(self, array, axis):
        if self.outer == 1:
            return array
        return lax.psum_scatter(
            array, "dp", scatter_dimension=axis, tiled=True, axis_index_groups=self.groups
        )


def cost(flops, moved, exps=0):
    return pl.CostEstimate(flops=int(flops), bytes_accessed=int(moved), transcendentals=int(exps))


def params():
    return pltpu.CompilerParams(vmem_limit_bytes=VMEM_BYTES)


def call(kernel, name, outs, ins, operands, *, grid=(1,), out_specs, scalars=None, scratch=(), work=None):
    if scalars is None:
        scalars = jnp.zeros((1,), jnp.int32)
    return pl.pallas_call(
        kernel,
        grid_spec=pltpu.PrefetchScalarGridSpec(
            num_scalar_prefetch=1, grid=grid, in_specs=ins, out_specs=out_specs, scratch_shapes=scratch
        ),
        out_shape=outs,
        compiler_params=params(),
        cost_estimate=work,
        name=name,
    )(scalars.astype(jnp.int32), *operands)


def full(shape):
    return pl.BlockSpec(shape, lambda *_: (0,) * len(shape))


def held(shape):
    return pl.BlockSpec(shape, lambda *_: (0,) * len(shape), pipeline_mode=pl.Buffered(1))


def shaped(shape, kind=BF16):
    return jax.ShapeDtypeStruct(shape, kind)


def unit_of(rows):
    centered = rows - jnp.mean(rows, axis=1, keepdims=True)
    inverse = lax.rsqrt(jnp.mean(centered * centered, axis=1, keepdims=True) + EPSILON)
    return centered * inverse, inverse


def norm_back(grad_rows, rows, scaling):
    unit, inverse = unit_of(rows)
    grad_unit = grad_rows * scaling
    centered = grad_unit - jnp.mean(grad_unit, axis=1, keepdims=True)
    slope = jnp.mean(grad_unit * unit, axis=1, keepdims=True)
    sums = (
        jnp.sum(grad_rows * unit, axis=0, keepdims=True),
        jnp.sum(grad_rows, axis=0, keepdims=True),
    )
    return inverse * (centered - unit * slope), sums


def norm_kernel(_, tokens_ref, gain_ref, bias_ref, out_ref):
    rows = tokens_ref[...].astype(F32)
    out_ref[...] = (unit_of(rows)[0] * gain_ref[...] + bias_ref[...]).astype(BF16)


def norm_rows(tokens, gain, bias):
    depth = tokens.shape[1]
    return call(
        norm_kernel,
        "norm_rows",
        shaped(tokens.shape),
        [full(tokens.shape), full((1, depth)), full((1, depth))],
        (tokens, gain[None], bias[None]),
        out_specs=full(tokens.shape),
        work=cost(0, 4 * tokens.size),
    )


def pack_kernel(s_ref, gate_ref, up_ref, down_ref, *targets):
    for k, target in enumerate(targets):
        at = pl.ds(pl.multiple_of((s_ref[0] ^ k) * 128, 128), 128)
        target[0] = gate_ref[:, at]
        target[1] = up_ref[:, at]
        target[2] = down_ref[at, :].astype(F32).T.astype(BF16)


def pack_hidden(gate, up, down, share):
    rows = gate.shape[0]
    block = (3, rows, 128)
    return call(
        pack_kernel,
        "pack_hidden",
        [shaped(block)] * BLOCK,
        [full(gate.shape), full(up.shape), full(down.shape)],
        (gate, up, down),
        out_specs=[full(block)] * BLOCK,
        scalars=jnp.reshape(share, (1,)),
        work=cost(0, 4 * 3 * gate.size),
    )


def place_hidden_kernel(s_ref, own, side, far, corner, inner_ref, down_ref):
    outer, _, rows, _ = inner_ref.shape
    for r in range(BLOCK):
        at = s_ref[0] ^ r
        for far_index, source in enumerate((own, far) if r < 4 else (side, corner)):
            for near_index in range(2):
                column = (far_index * 2 + near_index) * 128
                for matrix in range(3):
                    block = source[near_index * 4 + r % 4, matrix].reshape(outer, 1, rows, 128)
                    if matrix < 2:
                        first = matrix * 512 + column
                        inner_ref[:, pl.ds(at, 1), :, first : first + 128] = block
                    else:
                        down_ref[:, pl.ds(at, 1), :, column : column + 128] = block


def place_hidden(own, side, far, corner, base, outer):
    rows = own.shape[2]
    shapes = [(outer, BLOCK, rows // outer, width) for width in (1024, 512)]
    inner, down = call(
        place_hidden_kernel,
        "place_hidden",
        [shaped(shape) for shape in shapes],
        [full(own.shape)] * 4,
        (own, side, far, corner),
        out_specs=[full(shape) for shape in shapes],
        scalars=jnp.reshape(base, (1,)),
        work=cost(0, 4 * 4 * own.size),
    )
    return inner.reshape(BLOCK * rows, 1024), down.reshape(BLOCK * rows, 512)


def deliver_kernel(s_ref, *refs):
    sources, (gate_ref, up_ref, down_ref) = refs[:BLOCK], refs[BLOCK:]
    for k, source in enumerate(sources):
        at = pl.ds(pl.multiple_of((s_ref[0] ^ k) * 128, 128), 128)
        gate_ref[:, at] = source[:, 0:128].astype(F32)
        up_ref[:, at] = source[:, 128:256].astype(F32)
        down_ref[at, :] = source[:, 256:384].astype(F32).T


def deliver(sources, share):
    rows = sources[0].shape[0]
    shapes = [(rows, 1024), (rows, 1024), (1024, rows)]
    return call(
        deliver_kernel,
        "deliver",
        [shaped(shape, F32) for shape in shapes],
        [full((rows, 384))] * BLOCK,
        sources,
        out_specs=[full(shape) for shape in shapes],
        scalars=jnp.reshape(share, (1,)),
        work=cost(0, 6 * rows * 3072),
    )


def turned(values, lane):
    return jnp.where(lane % HEAD < HEAD // 2, pltpu.roll(values, 96, 1), pltpu.roll(values, 32, 1))


def project_kernel(s_ref, *refs):
    sources, quads, (cos_ref, sin_ref) = refs[:10], refs[10:14], refs[14:16]
    q_ref, k_ref, v_ref, kt_ref, vt_ref, h_ref, w_ref, buffer, arrived = refs[16:]
    step = pl.program_id(0)
    base = s_ref[4]
    width = q_ref.shape[1]

    def fetch(slot):
        choices = sources[2 * slot : 2 * slot + 2] if slot < 3 else sources[6:]
        for index, source in enumerate(choices):

            @pl.when(s_ref[5 + slot // 3] == index)
            def _(source=source):
                pltpu.make_async_copy(source, buffer.at[slot % 2], arrived.at[slot % 2]).start()

    @pl.when(step == 0)
    def _():
        fetch(0)
        outer, _, rows, _ = w_ref.shape
        for r in range(BLOCK):
            for part in range(3):
                block = quads[r // 2][r % 2, part].reshape(outer, 1, rows, width)
                w_ref[:, pl.ds(base ^ r, 1), :, part * width : (part + 1) * width] = block

    for slot in range(4):

        @pl.when(step == slot)
        def _(slot=slot):
            if slot < 3:
                fetch(slot + 1)
            here = buffer.at[slot % 2]
            pltpu.make_async_copy(sources[0], here, arrived.at[slot % 2]).wait()
            h_ref[...] = here[...]

    weight = w_ref[...].reshape(h_ref.shape[1], 3 * width)
    raw = dot(h_ref[...], weight, NN)
    cosine, sine = cos_ref[...], sin_ref[...]
    lane = lax.broadcasted_iota(jnp.int32, cosine.shape, 1)
    for target, first in ((q_ref, 0), (k_ref, width)):
        for column in range(0, width, 128):
            tile = raw[:, first + column : first + column + 128]
            turn = tile * cosine + turned(tile, lane) * sine
            target[:, column : column + 128] = turn.astype(BF16)
            if first:
                kt_ref[column : column + 128, :] = turn.T.astype(BF16)
    values = raw[:, 2 * width :]
    v_ref[...] = values.astype(BF16)
    vt_ref[...] = values.T.astype(BF16)


def project(sources, quads, cosine, sine, scalars, outer):
    step, depth = sources[0].shape
    _, _, rows, width = quads[0].shape
    narrow = pl.BlockSpec((step, width), lambda j, s: (s[j], 0))
    tall = pl.BlockSpec((width, step), lambda j, s: (0, s[j]))
    table = pl.BlockSpec((step, 128), lambda j, s: (s[j], 0))
    flat, deep = shaped((WIN, width)), shaped((width, WIN))
    weight = (outer, BLOCK, rows // outer, 3 * width)
    return call(
        project_kernel,
        "project",
        [flat, flat, flat, deep, deep, shaped((WIN, depth)), shaped(weight)],
        [pl.BlockSpec(memory_space=pl.ANY)] * 10 + [held(quads[0].shape)] * 4 + [table, table],
        (*sources, *quads, cosine, sine),
        grid=(4,),
        out_specs=[
            narrow,
            narrow,
            narrow,
            tall,
            tall,
            pl.BlockSpec((step, depth), lambda j, s: (s[j], 0)),
            full(weight),
        ],
        scalars=scalars,
        scratch=[pltpu.VMEM((2, step, depth), BF16), pltpu.SemaphoreType.DMA((2,))],
        work=cost(6 * WIN * depth * width, 6 * WIN * depth),
    )


def attend_kernel(_, q_ref, k_ref, vt_ref, bias_ref, *refs, step):
    outs, lse_ref = refs[:4], refs[4]
    rows = q_ref.shape[0]
    lane = lax.broadcasted_iota(jnp.int32, (rows, 128), 1)
    query = q_ref[...]
    mixed = []
    for head in range(2):
        own = (lane >= HEAD) == (head == 1)
        masked_query = jnp.where(own, query, jnp.zeros_like(query))
        place_v = slice(HEAD * head, HEAD * head + HEAD)
        top = None
        for first in range(0, WIN, step):
            keys = slice(first, first + step)
            scores = dot(k_ref[keys, :], masked_query, NT) * SCORE_LOG2 + bias_ref[keys, :1]
            block_top = jnp.max(scores, axis=0, keepdims=True)
            new_top = block_top if top is None else jnp.maximum(top, block_top)
            weights = jnp.exp2(scores - new_top)
            part = dot(vt_ref[place_v, keys], weights.astype(BF16), NN)
            part_sum = jnp.sum(weights, axis=0, keepdims=True)
            if top is None:
                sums, total = part, part_sum
            else:
                fade = jnp.exp2(top - new_top)
                sums, total = sums * fade + part, total * fade + part_sum
            top = new_top
        mixed.append(sums * (1.0 / total))
        lse_ref[0, head : head + 1, :] = top + jnp.log2(total)
    result = jnp.concatenate(mixed, axis=0).T.astype(BF16)
    chunk = outs[0].shape[0]
    per = rows // chunk
    for group in range(4 // per):

        @pl.when(pl.program_id(1) == group)
        def _(group=group):
            for index in range(per):
                outs[group * per + index][...] = result[index * chunk : (index + 1) * chunk]


def attend(query, key, value_t, bias, chunk, rows=1024, step=512):
    width = query.shape[1]
    pairs = width // 128
    return call(
        functools.partial(attend_kernel, step=step),
        "attend",
        [shaped((chunk, width))] * 4 + [shaped((pairs, 2, WIN), F32)],
        [
            pl.BlockSpec((rows, 128), lambda p, i, s: (i, p)),
            pl.BlockSpec((WIN, 128), lambda p, i, s: (0, p)),
            pl.BlockSpec((128, WIN), lambda p, i, s: (p, 0)),
            full((WIN, 128)),
        ],
        (query, key, value_t, bias),
        grid=(pairs, WIN // rows),
        out_specs=[pl.BlockSpec((chunk, 128), lambda p, i, s: (0, p))] * 4
        + [pl.BlockSpec((1, 2, rows), lambda p, i, s: (p, 0, i))],
        work=cost(16 * WIN * WIN * width, 8 * WIN * width, WIN * WIN * width // HEAD),
    )


def choose(refs, index):
    value = refs[0][...]
    for position, ref in enumerate(refs[1:], 1):
        value = jnp.where(index == position, ref[...], value)
    return value


def attend_back_kernel(_, q_ref, k_ref, v_ref, kt_ref, lse_ref, bias_ref, cosq_ref, sinq_ref,
                       cos_ref, sin_ref, *refs, step):
    mixed_refs, grad_refs = refs[:4], refs[4:8]
    dq_ref, dk_ref, dv_ref, dk_sum, dv_sum = refs[8:]
    rows = q_ref.shape[0]
    index = pl.program_id(0)

    @pl.when(index == 0)
    def _():
        dk_sum[...] = jnp.zeros_like(dk_sum)
        dv_sum[...] = jnp.zeros_like(dv_sum)

    lane = lax.broadcasted_iota(jnp.int32, (rows, 128), 1)
    query, grad = q_ref[...], choose(grad_refs, index)
    product = (grad.astype(F32) * choose(mixed_refs, index).astype(F32)).T
    grad_query = []
    for head in range(2):
        own = (lane >= HEAD) == (head == 1)
        masked_query = jnp.where(own, query, jnp.zeros_like(query))
        masked_grad = jnp.where(own, grad, jnp.zeros_like(grad))
        part = slice(HEAD * head, HEAD * head + HEAD)
        row_dot = jnp.sum(product[part, :], axis=0, keepdims=True)
        log_total = lse_ref[0, head : head + 1, :]
        sums = None
        for first in range(0, WIN, step):
            keys = slice(first, first + step)
            scores = dot(k_ref[keys, :], masked_query, NT) * SCORE_LOG2 + bias_ref[keys, :1]
            weights = jnp.exp2(scores - log_total)
            grad_weights = dot(v_ref[keys, :], masked_grad, NT)
            grad_scores = (weights * (grad_weights - row_dot)).astype(BF16)
            dv_sum[keys, :] += dot(weights.astype(BF16), masked_grad, NN)
            dk_sum[keys, :] += dot(grad_scores, masked_query, NN)
            more = dot(kt_ref[part, keys], grad_scores, NN)
            sums = more if sums is None else sums + more
        grad_query.append(sums)

    def unturn(values, cosine, sine):
        at = lax.broadcasted_iota(jnp.int32, values.shape, 1)
        return ((values * cosine - turned(values, at) * sine) * SCALE).astype(BF16)

    dq_ref[...] = unturn(jnp.concatenate(grad_query, axis=0).T, cosq_ref[...], sinq_ref[...])

    @pl.when(index == pl.num_programs(0) - 1)
    def _():
        dk_ref[...] = unturn(dk_sum[...], cos_ref[...], sin_ref[...])
        dv_ref[...] = dv_sum[...].astype(BF16)


def attend_back(pair, query, key, value, key_t, mixed, grad, lse, bias, cosine, sine, step=512):
    rows = grad[0].shape[0]
    block = pl.BlockSpec((rows, 128), lambda i, s: (i, pair))
    piece = pl.BlockSpec((rows, 128), lambda i, s: (0, pair))
    whole = pl.BlockSpec((WIN, 128), lambda i, s: (0, pair))
    local = pl.BlockSpec((rows, 128), lambda i, s: (i, 0))
    return call(
        functools.partial(attend_back_kernel, step=step),
        "attend_back",
        [shaped((WIN, 128))] * 3,
        [
            block,
            whole,
            whole,
            pl.BlockSpec((128, WIN), lambda i, s: (pair, 0)),
            pl.BlockSpec((1, 2, rows), lambda i, s: (pair, 0, i)),
            full((WIN, 128)),
            local,
            local,
            full((WIN, 128)),
            full((WIN, 128)),
        ]
        + [piece] * 8,
        (query, key, value, key_t, lse, bias, cosine, sine, cosine, sine, *mixed, *grad),
        grid=(WIN // rows,),
        out_specs=[local, full((WIN, 128)), full((WIN, 128))],
        scratch=[pltpu.VMEM((WIN, 128), F32)] * 2,
        work=cost(40 * WIN * WIN * 128, 16 * WIN * 128, WIN * WIN * 2),
    )


def unproject_kernel(_, *refs):
    grads, (weight_ref, out_ref) = refs[:-2], refs[-2:]
    grad = jnp.concatenate([ref[...] for ref in grads], axis=1)
    out_ref[...] = dot(grad, weight_ref[...], NT).astype(BF16)


def unproject(grads, weight, scalars, slot):
    depth, triple = weight.shape
    step = WIN // 4
    spec = pl.BlockSpec((step, 128), lambda j, s: (s[slot], 0))
    return call(
        unproject_kernel,
        "unproject",
        shaped((step, depth)),
        [spec] * len(grads) + [full((depth, triple))],
        (*grads, weight),
        out_specs=full((step, depth)),
        scalars=scalars,
        work=cost(2 * step * depth * triple, 4 * step * depth),
    )


def weight_grad_kernel(s_ref, rows_ref, *refs):
    grads, out_ref = refs[:-1], refs[-1]
    grad = jnp.concatenate([ref[...] for ref in grads], axis=1)
    total = dot(rows_ref[...], grad, TN).astype(BF16)
    part = pl.program_id(0)
    rows = out_ref.shape[1]
    count = total.shape[0] // rows
    for index in range(count):
        out_ref[s_ref[4] ^ (part * count + index)] = total[index * rows : (index + 1) * rows]


def weight_grad(rows, grads, scalars):
    depth, triple = rows.shape[1], 128 * len(grads)
    parts = 2
    out = (BLOCK, depth // BLOCK, triple)
    return call(
        weight_grad_kernel,
        "weight_grad",
        shaped(out),
        [pl.BlockSpec((WIN, depth // parts), lambda j, s: (0, j))] + [held((WIN, 128))] * len(grads),
        (rows, *grads),
        grid=(parts,),
        out_specs=full(out),
        scalars=scalars,
        work=cost(2 * WIN * depth * triple, 4 * WIN * depth),
    )


def out_norm_kernel(s_ref, m0, m1, m2, m3, own_ref, other_ref, tokens_ref, gain_ref, bias_ref,
                    residual_ref, normed_ref, weight_ref):
    outer, _, rows, _ = weight_ref.shape
    width = m0.shape[1]

    @pl.when(pl.program_id(0) == 0)
    def _():
        for r in range(BLOCK):
            source = own_ref if r % 2 == 0 else other_ref
            for group in range(4):
                block = source[r // 2, group].reshape(outer, 1, rows, width)
                columns = slice(group * width, (group + 1) * width)
                weight_ref[:, pl.ds(s_ref[0] ^ r, 1), :, columns] = block

    weight = weight_ref[...].reshape(residual_ref.shape[1], 4 * width)
    mixed = jnp.concatenate([ref[...] for ref in (m0, m1, m2, m3)], axis=1)
    residual = tokens_ref[...].astype(F32) + dot(mixed, weight, NT)
    residual_ref[...] = residual
    normed_ref[...] = (unit_of(residual)[0] * gain_ref[...] + bias_ref[...]).astype(BF16)


def out_norm(mixed, own, other, tokens, gain, bias, inner, outer):
    chunk, width = mixed[0].shape
    depth = tokens.shape[1]
    step = chunk // 2
    rows = own.shape[2]
    weight = (outer, BLOCK, rows // outer, 4 * width)
    by_rows = pl.BlockSpec((step, depth), lambda j, s: (j, 0))
    residual, normed, placed = call(
        out_norm_kernel,
        "out_norm",
        [shaped(tokens.shape, F32), shaped(tokens.shape), shaped(weight)],
        [pl.BlockSpec((step, width), lambda j, s: (j, 0))] * 4
        + [held(own.shape)] * 2
        + [by_rows, full((1, depth)), full((1, depth))],
        (*mixed, own, other, tokens, gain[None], bias[None]),
        grid=(2,),
        out_specs=[by_rows, by_rows, full(weight)],
        scalars=jnp.reshape(inner, (1,)),
        work=cost(2 * chunk * depth * depth, 12 * tokens.size),
    )
    return residual, normed, placed.reshape(depth, 4 * width)


def middle_back_kernel(_, own_ref, own2_ref, side_ref, near_ref, corner_ref, cot_ref, residual_ref,
                       gain_ref, weight_ref, grad_ref, low_ref, g0, g1, g2, g3, sums_ref):
    step = pl.program_id(0)
    grad_rows = own_ref[...].astype(F32)
    for ref in (own2_ref, side_ref, near_ref, corner_ref):
        grad_rows = grad_rows + ref[...].astype(F32)
    change, sums = norm_back(grad_rows, residual_ref[...], gain_ref[...])
    grad = cot_ref[...].astype(F32) + change
    grad_ref[...] = grad
    low = grad.astype(BF16)
    low_ref[...] = low
    back = dot(low, weight_ref[...], NN).astype(BF16)
    width = g0.shape[1]
    for k, ref in enumerate((g0, g1, g2, g3)):
        ref[...] = back[:, k * width : (k + 1) * width]

    @pl.when(step == 0)
    def _():
        sums_ref[...] = jnp.zeros_like(sums_ref)

    sums_ref[0:1, :] += sums[0]
    sums_ref[1:2, :] += sums[1]


def middle_back(parts, cotangent, residual, gain, weight):
    rows, depth = cotangent.shape
    width = depth // 4
    step = rows // 2
    by_rows = pl.BlockSpec((step, depth), lambda j, s: (j, 0))
    narrow = pl.BlockSpec((step, width), lambda j, s: (j, 0))
    return call(
        middle_back_kernel,
        "middle_back",
        [shaped((rows, depth), F32), shaped((rows, depth))]
        + [shaped((rows, width))] * 4
        + [shaped((2, depth), F32)],
        [by_rows] * 7 + [full((1, depth)), held(weight.shape)],
        (*parts, cotangent, residual, gain[None], weight),
        grid=(2,),
        out_specs=[by_rows, by_rows] + [narrow] * 4 + [full((2, depth))],
        work=cost(2 * rows * depth * depth, 24 * rows * depth),
    )


def out_grad_kernel(s_ref, low_ref, m0, m1, m2, m3, keep_ref, give_ref):
    mixed = jnp.concatenate([ref[...] for ref in (m0, m1, m2, m3)], axis=1)
    total = dot(low_ref[...], mixed, TN).astype(BF16)
    rows = keep_ref.shape[1]
    for index in range(BLOCK):
        block = total[index * rows : (index + 1) * rows]
        place = s_ref[0] ^ index

        @pl.when(place % 2 == 0)
        def _(block=block, place=place):
            keep_ref[place // 2] = block

        @pl.when(place % 2 == 1)
        def _(block=block, place=place):
            give_ref[place // 2] = block


def out_grad_blocks(low, mixed, inner):
    rows, depth = low.shape
    width = mixed[0].shape[1]
    out = (4, depth // BLOCK, 4 * width)
    return call(
        out_grad_kernel,
        "out_grad",
        [shaped(out)] * 2,
        [full(low.shape)] + [full((rows, width))] * 4,
        (low, *mixed),
        out_specs=[full(out)] * 2,
        scalars=jnp.reshape(inner, (1,)),
        work=cost(2 * rows * depth * depth, 6 * rows * depth),
    )


def first_back_kernel(s_ref, sent_ref, end_ref, own_ref, got_ref, grad_ref, tokens_ref, gain_ref,
                      out_ref, sums_ref):
    own = jnp.where(s_ref[0] == 1, own_ref[...].astype(F32) + got_ref[...].astype(F32), 0.0)
    end = jnp.where(s_ref[1] == 1, end_ref[...].astype(F32), 0.0)
    grad_rows = sent_ref[...].astype(F32) + own + end
    change, sums = norm_back(grad_rows, tokens_ref[...].astype(F32), gain_ref[...])
    out_ref[...] = (grad_ref[...] + change).astype(BF16)

    @pl.when(pl.program_id(0) == 0)
    def _():
        sums_ref[...] = jnp.zeros_like(sums_ref)

    sums_ref[0:1, :] += sums[0]
    sums_ref[1:2, :] += sums[1]


def first_back(parts, grad, tokens, gain, flags):
    rows, depth = tokens.shape
    by_rows = pl.BlockSpec((rows // 2, depth), lambda j, s: (j, 0))
    return call(
        first_back_kernel,
        "first_back",
        [shaped(tokens.shape), shaped((2, depth), F32)],
        [by_rows] * 6 + [full((1, depth))],
        (*parts, grad, tokens, gain[None]),
        grid=(2,),
        out_specs=[by_rows, full((2, depth))],
        scalars=flags,
        work=cost(0, 16 * tokens.size),
    )


def hidden_back_kernel(_, a_ref, b_ref, down_ref, out_ref):
    step = pl.program_id(0)
    rows = jnp.where(step == 0, a_ref[...], b_ref[...])
    out_ref[...] = dot(rows, down_ref[...], NN).astype(BF16)


def hidden_back(pair, down):
    rows, depth = pair[0].shape
    hidden = down.shape[1]
    return call(
        hidden_back_kernel,
        "hidden_back",
        shaped((2 * rows, hidden)),
        [full((rows, depth))] * 2 + [held(down.shape)],
        (*pair, down),
        grid=(2,),
        out_specs=pl.BlockSpec((rows, hidden), lambda j, s: (j, 0)),
        work=cost(4 * rows * depth * hidden, 4 * rows * depth),
    )


def feed_kernel(_, a_ref, b_ref, grad_ref, inner_ref, down_ref,
                hidden_ref, both_ref, back_ref, out_ref, other_ref):
    step = pl.program_id(0)
    width = down_ref.shape[1]
    depth = a_ref.shape[1]
    rows = jnp.where(step == 0, a_ref[...], b_ref[...])
    gate = dot(rows, inner_ref[:, :width], NN)
    up = dot(rows, inner_ref[:, width:], NN)
    sigmoid = 1.0 / (1.0 + jnp.exp(-gate))
    activated = gate * sigmoid
    hidden = (activated * up).astype(BF16)
    hidden_ref[...] = hidden
    grad = grad_ref[...].astype(F32)
    grad_gate = (grad * up * sigmoid * (1.0 + gate * (1.0 - sigmoid))).astype(BF16)
    grad_up = (grad * activated).astype(BF16)
    both_ref[:, :width] = grad_gate
    both_ref[:, width:] = grad_up
    back = dot(grad_gate, inner_ref[:, :width], NT) + dot(grad_up, inner_ref[:, width:], NT)
    out = dot(hidden, down_ref[...], NT)

    @pl.when(step == 0)
    def _():
        back_ref[...] = back.astype(BF16)
        out_ref[...] = out.astype(BF16)

    @pl.when(step == 1)
    def _():
        other_ref[:, :depth] = back.astype(BF16)
        other_ref[:, depth:] = out.astype(BF16)


def feed(pair, grad, inner, down):
    rows, depth = pair[0].shape
    hidden = down.shape[1]
    return call(
        feed_kernel,
        "feed",
        [
            shaped((2 * rows, hidden)),
            shaped((2 * rows, 2 * hidden)),
            shaped((rows, depth)),
            shaped((rows, depth)),
            shaped((rows, 2 * depth)),
        ],
        [full((rows, depth))] * 2
        + [pl.BlockSpec((rows, hidden), lambda j, s: (j, 0)), held(inner.shape), held(down.shape)],
        (*pair, grad, inner, down),
        grid=(2,),
        out_specs=[
            pl.BlockSpec((rows, hidden), lambda j, s: (j, 0)),
            pl.BlockSpec((rows, 2 * hidden), lambda j, s: (j, 0)),
            full((rows, depth)),
            full((rows, depth)),
            full((rows, 2 * depth)),
        ],
        work=cost(20 * rows * depth * hidden, 12 * rows * depth),
    )


def hidden_grad_kernel(s_ref, *refs):
    rows, cots, both, hiddens = refs[:8], refs[8:16], refs[16:20], refs[20:24]
    out_ref, total, *buffers, arrived = refs[24:]
    size, half = buffers[0].shape[1:]
    width = hiddens[0].shape[1]
    columns = pl.ds(pl.multiple_of(s_ref[0] * half, half), half)

    def copies(index):
        at = pl.ds(index % 2 * size, size)
        sources = (
            rows[index].at[:, columns],
            cots[index].at[:, columns],
            both[index // 2].at[at, :],
            hiddens[index // 2].at[at, :],
        )
        return [
            pltpu.make_async_copy(source, buffer.at[index % 2], arrived.at[index % 2, number])
            for number, (source, buffer) in enumerate(zip(sources, buffers, strict=True))
        ]

    for copy in copies(0):
        copy.start()
    for index in range(8):
        if index < 7:
            for copy in copies(index + 1):
                copy.start()
        for copy in copies(index):
            copy.wait()
        row, cot, grad, hidden = (buffer[index % 2] for buffer in buffers)
        inner = dot(row, grad, TN)
        down = dot(cot, hidden, TN)
        if index == 0:
            total[:, : 2 * width] = inner
            total[:, 2 * width :] = down
        else:
            total[:, : 2 * width] += inner
            total[:, 2 * width :] += down
    for block in range(half // 128):
        for column in range(4):
            for matrix in range(3):
                first = matrix * width + column * 128
                last = (column * 3 + matrix) * 128
                out_ref[block ^ s_ref[1], :, last : last + 128] = total[
                    block * 128 : (block + 1) * 128, first : first + 128
                ].astype(BF16)


def hidden_grads(rows, cots, both, hiddens, scalars):
    size, depth = rows[0].shape
    width = hiddens[0].shape[1]
    half = depth // 2
    out = (4, 128, 3 * width)
    return call(
        hidden_grad_kernel,
        "hidden_grads",
        shaped(out),
        [pl.BlockSpec(memory_space=pl.ANY)] * 24,
        (*rows, *cots, *both, *hiddens),
        out_specs=full(out),
        scalars=scalars,
        scratch=[
            pltpu.VMEM((half, 3 * width), F32),
            pltpu.VMEM((2, size, half), BF16),
            pltpu.VMEM((2, size, half), BF16),
            pltpu.VMEM((2, size, 2 * width), BF16),
            pltpu.VMEM((2, size, width), BF16),
            pltpu.SemaphoreType.DMA((2, 4)),
        ],
        work=cost(24 * size * depth * width, 20 * size * depth),
    )


def split_kernel(_, a_ref, b_ref, *targets):
    width = targets[0].shape[1]
    for k, target in enumerate(targets):
        block, column = k % 4, slice(k // 4 * width, (k // 4 + 1) * width)
        total = a_ref[block, :, column].astype(F32) + b_ref[block, :, column].astype(F32)
        target[...] = total.astype(BF16)


def split(left, right):
    _, rows, double = left.shape
    out = (rows, double // 2)
    return call(
        split_kernel,
        "split",
        [shaped(out)] * BLOCK,
        [full(left.shape), full(right.shape)],
        (left, right),
        out_specs=[full(out)] * BLOCK,
        work=cost(0, 6 * left.size),
    )


def add(*arrays):
    total = arrays[0].astype(F32)
    for array in arrays[1:]:
        total = total + array.astype(F32)
    return total.astype(BF16)


def after(value, *others):
    return lax.optimization_barrier((value, *others))[0]


def collect_window(links, own):
    first = links.move(own, lambda d, t: ((d, t + 1) if t < 3 else None) if d & 1 else ((d, t - 1) if t else None))
    end = links.move(own, lambda d, t: {(0, 0): (d ^ 1, 1), (1, 3): (d ^ 1, 2)}.get((d & 1, t)))
    second = links.move(
        first,
        lambda d, t: {(0, 2): (d, 1), (0, 1): (d, 0), (1, 1): (d, 2), (1, 2): (d, 3)}.get((d & 1, t)),
    )
    third = links.move(second, lambda d, t: {(0, 1): (d, 0), (1, 2): (d, 3)}.get((d & 1, t)))

    def lend(array):
        return links.move(array, lambda d, t: (d ^ 1, t) if (d & 1) == t // 2 else None)

    end_lent = links.move(end, lambda d, t: {(1, 1): (d ^ 1, t), (0, 2): (d ^ 1, t)}.get((d & 1, t)))
    sources = [own, lend(own), first, lend(first), second, lend(second), third, lend(third), end_lent, end]
    return sources, first, second, third


def return_window(links, parts, owned, line):
    got = [links.swap(part, CORE) for part in parts[::-1]][::-1]
    end = links.move(
        add(parts[3], got[3]),
        lambda d, t: {
            (0, 0): (d, 1),
            (1, 3): (d, 2),
            (1, 1): (d ^ 1, 0),
            (0, 2): (d ^ 1, 3),
        }.get((d & 1, t)),
    )
    inside = (line == 1) | (line == 2)
    zero = jnp.zeros((), BF16)
    second = links.move(
        add(parts[2], got[2], jnp.where(inside, end, zero)),
        lambda d, t: {(0, 1): (d, 2), (0, 0): (d, 1), (1, 2): (d, 1), (1, 3): (d, 2)}.get((d & 1, t)),
    )
    first = links.move(
        add(second, jnp.where(owned, parts[1], zero), jnp.where(owned, got[1], zero)),
        lambda d, t: ((d, t - 1) if t else None) if d & 1 else ((d, t + 1) if t < 3 else None),
    )
    return first, end, parts[0], got[0]


def collect_block(links, rows):
    half = rows.shape[0] // 2
    side, near = links.swap(rows, SIDE), links.swap(rows, NEAR)
    corner = jnp.concatenate(
        [links.swap(near[:half], SIDE), links.swap(side[half:], NEAR)], axis=0
    )
    return [(part, links.swap(part, CORE)) for part in (rows, side, near, corner)]


def collect_block_late(links, rows, gate):
    side = links.swap(rows, SIDE)
    near = links.swap(after(rows, gate), NEAR)
    corner = links.swap(near, SIDE)
    return [(part, links.swap(part, CORE)) for part in (rows, side, near, corner)]


def per_device(
    links,
    tokens,
    lengths,
    cotangent,
    attention_gain,
    attention_bias,
    query_weight,
    key_weight,
    value_weight,
    out_weight,
    feedforward_gain,
    feedforward_bias,
    gate_weight,
    up_weight,
    down_weight,
):
    outer = links.outer
    dp = lax.axis_index("dp")
    line = lax.axis_index("tensor")
    core, inner = dp % 2, dp % BLOCK
    side_bit, far_bit = dp // 2 % 2, dp // 4 % 2
    near_bit = line % 2
    window = line // 2
    share = near_bit * 2 + core
    hidden_share = near_bit * 4 + side_bit * 2 + core
    width = query_weight.shape[1]
    chunk, depth = tokens.shape

    def by_block(array):
        if outer == 1:
            return array
        shape = (array.shape[0], outer, BLOCK, depth // (outer * BLOCK))
        return array.reshape(shape).transpose(0, 2, 1, 3).reshape(array.shape)

    qkv = links.gather_outer(jnp.stack([query_weight, key_weight, value_weight]), 1)
    pair = jnp.stack(
        [
            links.move(
                qkv, lambda d, t, k=k: ((d & ~1) | (t % 2), t // 2 + 2 * ((d & 1) ^ k))
            )
            for k in range(2)
        ]
    )
    corner_mask = (SIDE[0] | FAR_SIDE[0], 0)
    quads = [pair] + [links.swap(pair, mask) for mask in (SIDE, FAR_SIDE, corner_mask)]

    normed_first = norm_rows(tokens, attention_gain, attention_bias)
    sources, first_round, second_round, last_round = collect_window(links, normed_first)

    order_chunk = jnp.arange(4, dtype=jnp.int32) ^ share
    positions = (order_chunk[:, None] * chunk + jnp.arange(chunk, dtype=jnp.int32)).reshape(-1)
    lane = jnp.arange(128, dtype=jnp.int32)
    frequency = jnp.power(ROTARY_BASE, -(lane % (HEAD // 2)).astype(F32) * 2.0 / HEAD)
    angles = positions.astype(F32)[:, None] * frequency[None, :]
    cosine = jnp.cos(angles)
    sine = jnp.sin(angles) * jnp.where(lane % HEAD < HEAD // 2, -1.0, 1.0)
    length = jnp.where(core == window, lengths, links.swap(lengths, CORE))
    bias = jnp.where(positions < length[0], 0.0, MASKED).astype(F32)
    bias = jnp.broadcast_to(bias[:, None], (WIN, 128))
    slot = jnp.arange(4, dtype=jnp.int32)
    slot_chunk = jnp.where(line < 2, line + slot, line - slot) % 4
    owned = core == window
    ends = (line == 0) | (line == 3)
    last_source = jnp.where(ends, 1 - owned.astype(jnp.int32), 3 - owned.astype(jnp.int32))
    scalars = jnp.concatenate(
        [
            slot_chunk ^ share,
            jnp.stack([(inner // 2) * 2 + window, 1 - owned.astype(jnp.int32), last_source]),
        ]
    ).astype(jnp.int32)

    piece = links.gather_outer(out_weight.T, 0)
    piece = after(piece, first_round)
    both_mask = (0, NEAR[1] | FAR[1])
    line_pieces = jnp.stack([piece] + [links.swap(piece, mask) for mask in (NEAR, FAR, both_mask)])
    out_own = jnp.stack(
        [line_pieces] + [links.swap(line_pieces, mask) for mask in (SIDE, FAR_SIDE, corner_mask)]
    )
    out_other = links.swap(out_own, CORE)

    blocks = pack_hidden(
        links.gather_outer(gate_weight, 0),
        links.gather_outer(up_weight, 0),
        links.gather_outer(down_weight, 1),
        hidden_share,
    )
    blocks = lax.optimization_barrier((*blocks, second_round))[:BLOCK]
    mine = jnp.stack(
        [blocks[0]]
        + [
            links.swap(
                blocks[k],
                ((SIDE[0] if k & 2 else 0) | (k & 1), NEAR[1] if k & 4 else 0),
            )
            for k in range(1, BLOCK)
        ]
    )
    far = links.swap(after(mine, last_round), FAR)
    weight_in, weight_down = place_hidden(
        mine, links.swap(mine, FAR_SIDE), far, links.swap(far, FAR_SIDE), inner, outer
    )
    cots = collect_block_late(links, cotangent, last_round)

    query, key, value, key_t, value_t, rows_first, weight_qkv = project(
        sources, quads, cosine, sine, scalars, outer
    )
    *mixed, lse = attend(query, key, value_t, bias, chunk)

    def to_owner(k):
        def rule(d, t):
            return (d & ~1) | (t // 2), ((t % 2) * 2 + (d & 1)) ^ k

        return rule

    def to_heads(k):
        def rule(d, t):
            who = t ^ k
            return (d & ~1) | (who & 1), (who >> 1) + 2 * (d & 1)

        return rule

    attended = [links.move(mixed[k], to_owner(k)) for k in range(4)]
    grad_hidden = [hidden_back(cot, weight_down) for cot in cots]
    residual, normed_second, weight_out = out_norm(
        attended, out_own, out_other, tokens, feedforward_gain, feedforward_bias, inner, outer
    )
    rows = collect_block(links, normed_second)

    fed = [
        feed(pair_rows, grad, weight_in, weight_down)
        for pair_rows, grad in zip(rows, grad_hidden, strict=True)
    ]
    hiddens, boths, backs, outs, others = zip(*fed, strict=True)
    others = [links.swap(other, CORE) for other in others]

    def hidden_half(index):
        flat = [part for pair_rows in rows for part in pair_rows]
        flat_cots = [part for cot in cots for part in cot]
        if outer > 1:
            flat = [by_block(part) for part in flat]
            flat_cots = [by_block(part) for part in flat_cots]
        where = jnp.stack([index, side_bit * 2 + core])
        return hidden_grads(flat, flat_cots, boths, hiddens, where)

    corner_near = (SIDE[0], NEAR[1])
    masks = (SIDE, NEAR, corner_near)
    back_sent = [
        links.swap(add(backs[q], others[q][:, :depth]), masks[q - 1]) for q in range(1, 4)
    ]
    hidden_given = hidden_half(1 - far_bit)
    hidden_got = links.swap(hidden_given, FAR_SIDE)
    grad_residual, grad_attn, *grad_attended, sums_second = middle_back(
        (backs[0], others[0][:, :depth], *back_sent),
        after(cotangent, hidden_given),
        residual,
        feedforward_gain,
        weight_out,
    )
    grad_mixed = [links.move(grad_attended[k], to_heads(k)) for k in range(4)]

    out_sent = [
        links.swap(after(add(outs[q], others[q][:, depth:]), grad_attn), masks[q - 1])
        for q in range(1, 4)
    ]
    layer_out = (
        residual
        + outs[0].astype(F32)
        + others[0][:, depth:].astype(F32)
        + out_sent[0].astype(F32)
        + out_sent[1].astype(F32)
        + out_sent[2].astype(F32)
    ).astype(BF16)

    kept, given = out_grad_blocks(by_block(grad_attn), attended, inner)
    sums = add(kept, links.swap(given, CORE))
    sums = add(
        sums[0], *(links.swap(sums[q], mask) for q, mask in ((1, SIDE), (2, FAR_SIDE), (3, corner_mask)))
    )
    sums = add(
        sums[:, :width],
        *(
            links.swap(sums[:, q * width : (q + 1) * width], mask)
            for q, mask in ((1, NEAR), (2, FAR), (3, both_mask))
        ),
    )
    out_grad = links.scatter_outer(sums, 0).astype(F32).T

    hidden_kept = hidden_half(far_bit)
    sums = add(hidden_kept, hidden_got)
    half = sums.shape[2] // 2
    near_part, far_part = sums[:, :, :half], sums[:, :, half:]
    far_got = links.swap(far_part, FAR)
    grad_mixed[0] = after(grad_mixed[0], near_part)
    terms = (query, key, value, key_t, mixed, grad_mixed, lse, bias, cosine, sine)
    back_first = attend_back(0, *terms)
    parts = split(after(near_part, back_first[0]), far_got)
    back_second = attend_back(1, after(query, parts[0]), *terms[1:])
    parts = [parts[0]] + [
        links.swap(parts[k], ((SIDE[0] if k & 2 else 0) | (k & 1), NEAR[1] if k & 4 else 0))
        for k in range(1, BLOCK)
    ]
    parts = [links.scatter_outer(part, 0) for part in parts]
    gate_grad, up_grad, down_grad = deliver(parts, hidden_share)

    grads = [part for both in zip(back_first, back_second, strict=True) for part in both]
    weight_qkv = weight_qkv.reshape(depth, 3 * width)
    sums = [None] * 4
    for slot in (3, 2, 1, 0):
        sums[slot] = unproject(grads, weight_qkv, scalars, slot)
    tokens_grad, sums_first = first_back(
        return_window(links, sums, owned, line),
        grad_residual,
        tokens,
        attention_gain,
        jnp.stack([owned, ends]),
    )

    blocks = weight_grad(by_block(rows_first), grads, scalars)
    blocks = blocks.reshape(4, 2 * (depth // BLOCK), 3 * width)
    sums = add(
        blocks[0],
        *(links.swap(blocks[q], mask) for q, mask in ((1, SIDE), (2, FAR_SIDE), (3, corner_mask))),
    )
    rows_each = depth // BLOCK
    halves = [
        links.move(
            sums[k * rows_each : (k + 1) * rows_each],
            lambda d, t, k=k: ((d & ~1) | ((t // 2) ^ k), (t % 2) * 2 + (d & 1)),
        )
        for k in range(2)
    ]
    sums = links.scatter_outer(add(*halves), 0).astype(F32)

    norms = jnp.concatenate([sums_first, sums_second], axis=0)
    side, far, corner = (links.swap(norms, mask) for mask in (SIDE, FAR_SIDE, corner_mask))
    norms = (norms + side) + (far + corner)
    near, far, both = (links.swap(norms, mask) for mask in (NEAR, FAR, both_mask))
    norms = (norms + near) + (far + both)
    norms = norms + links.swap(norms, CORE)
    for bit in range(3, links.nd.bit_length() - 1):
        norms = norms + links.swap(norms, (1 << bit, 0))
    return (
        layer_out,
        tokens_grad,
        norms[0],
        norms[1],
        sums[:, :width],
        sums[:, width : 2 * width],
        sums[:, 2 * width :],
        out_grad,
        norms[2],
        norms[3],
        gate_grad,
        up_grad,
        down_grad,
    )


def solution(mesh):
    rows, columns = P("dp", "tensor"), P("tensor", "dp")
    spread = P(("dp", "tensor"), None)
    placed = (
        spread, P("dp"), spread, P(), P(), rows, rows, rows, columns, P(), P(), rows, rows, columns
    )
    given = (
        spread, spread, P(), P(), rows, rows, rows, columns, P(), P(), rows, rows, columns
    )
    return jax.shard_map(
        functools.partial(per_device, Links(mesh)),
        mesh=mesh,
        in_specs=placed,
        out_specs=given,
        check_vma=False,
    )
```

```python
import functools
import math

import jax
import jax.numpy as jnp
from jax import lax
from jax.experimental import pallas as pl
from jax.experimental.pallas import tpu as pltpu
from jax.sharding import PartitionSpec as P

HEAD = 64
WIN = 2048
EPSILON = 1e-05
MASKED = -1000000000.0
ROTARY_BASE = 10000.0
SCALE = 1.0 / math.sqrt(HEAD)
SCORE_LOG2 = SCALE * math.log2(math.e)

BLOCK = 8
CORE = (1, 0)
SIDE = (2, 0)
FAR_SIDE = (4, 0)
NEAR = (0, 1)
FAR = (0, 2)

F32 = jnp.float32
BF16 = jnp.bfloat16
NT = (((1,), (1,)), ((), ()))
NN = (((1,), (0,)), ((), ()))
TN = (((0,), (0,)), ((), ()))
VMEM_BYTES = 56 * 1024 * 1024


def dot(left, right, dims):
    return lax.dot_general(left, right, dims, preferred_element_type=F32)


def pick(array, index, axis):
    return lax.dynamic_index_in_dim(array, index, axis, keepdims=False)


class Links:
    def __init__(self, mesh):
        self.nd = mesh.shape["dp"]
        self.nt = mesh.shape["tensor"]
        self.outer = self.nd // BLOCK
        self.groups = [[o * BLOCK + i for o in range(self.outer)] for i in range(BLOCK)]

    def move(self, array, rule):
        pairs = []
        for d in range(self.nd):
            for t in range(self.nt):
                target = rule(d, t)
                if target is not None:
                    pairs.append((d * self.nt + t, target[0] * self.nt + target[1]))
        return lax.ppermute(array, ("dp", "tensor"), pairs)

    def swap(self, array, mask):
        return self.move(array, lambda d, t: (d ^ mask[0], t ^ mask[1]))

    def gather_outer(self, array, axis):
        if self.outer == 1:
            return array
        return lax.all_gather(array, "dp", axis=axis, tiled=True, axis_index_groups=self.groups)

    def scatter_outer(self, array, axis):
        if self.outer == 1:
            return array
        return lax.psum_scatter(
            array, "dp", scatter_dimension=axis, tiled=True, axis_index_groups=self.groups
        )


COST = 3


def cost(flops, moved, exps=0):
    return pl.CostEstimate(
        flops=int(COST * flops), bytes_accessed=int(COST * moved), transcendentals=int(COST * exps)
    )


def params():
    return pltpu.CompilerParams(vmem_limit_bytes=VMEM_BYTES)


def call(kernel, name, outs, ins, operands, *, grid=(1,), out_specs, scalars=None, scratch=(), work=None):
    if scalars is None:
        scalars = jnp.zeros((1,), jnp.int32)
    return pl.pallas_call(
        kernel,
        grid_spec=pltpu.PrefetchScalarGridSpec(
            num_scalar_prefetch=1, grid=grid, in_specs=ins, out_specs=out_specs, scratch_shapes=scratch
        ),
        out_shape=outs,
        compiler_params=params(),
        cost_estimate=work,
        name=name,
    )(scalars.astype(jnp.int32), *operands)


def full(shape):
    return pl.BlockSpec(shape, lambda *_: (0,) * len(shape))


def held(shape):
    return pl.BlockSpec(shape, lambda *_: (0,) * len(shape), pipeline_mode=pl.Buffered(1))


def shaped(shape, kind=BF16):
    return jax.ShapeDtypeStruct(shape, kind)


def unit_of(rows):
    centered = rows - jnp.mean(rows, axis=1, keepdims=True)
    inverse = lax.rsqrt(jnp.mean(centered * centered, axis=1, keepdims=True) + EPSILON)
    return centered * inverse, inverse


def norm_back(grad_rows, rows, scaling):
    unit, inverse = unit_of(rows)
    grad_unit = grad_rows * scaling
    centered = grad_unit - jnp.mean(grad_unit, axis=1, keepdims=True)
    slope = jnp.mean(grad_unit * unit, axis=1, keepdims=True)
    sums = (
        jnp.sum(grad_rows * unit, axis=0, keepdims=True),
        jnp.sum(grad_rows, axis=0, keepdims=True),
    )
    return inverse * (centered - unit * slope), sums


def norm_kernel(_, tokens_ref, gain_ref, bias_ref, out_ref):
    rows = tokens_ref[...].astype(F32)
    out_ref[...] = (unit_of(rows)[0] * gain_ref[...] + bias_ref[...]).astype(BF16)


def norm_rows(tokens, gain, bias):
    depth = tokens.shape[1]
    return call(
        norm_kernel,
        "norm_rows",
        shaped(tokens.shape),
        [full(tokens.shape), full((1, depth)), full((1, depth))],
        (tokens, gain[None], bias[None]),
        out_specs=full(tokens.shape),
        work=cost(0, 4 * tokens.size),
    )


def pack_kernel(s_ref, gate_ref, up_ref, down_ref, *targets):
    for k, target in enumerate(targets):
        at = pl.ds(pl.multiple_of((s_ref[0] ^ k) * 128, 128), 128)
        target[0] = gate_ref[:, at]
        target[1] = up_ref[:, at]
        target[2] = down_ref[at, :].astype(F32).T.astype(BF16)


def pack_hidden(gate, up, down, share):
    rows = gate.shape[0]
    block = (3, rows, 128)
    return call(
        pack_kernel,
        "pack_hidden",
        [shaped(block)] * BLOCK,
        [full(gate.shape), full(up.shape), full(down.shape)],
        (gate, up, down),
        out_specs=[full(block)] * BLOCK,
        scalars=jnp.reshape(share, (1,)),
        work=cost(0, 4 * 3 * gate.size),
    )


def place_hidden_kernel(s_ref, own, side, far, corner, inner_ref, down_ref):
    outer, _, rows, _ = inner_ref.shape
    for r in range(BLOCK):
        at = s_ref[0] ^ r
        for far_index, source in enumerate((own, far) if r < 4 else (side, corner)):
            for near_index in range(2):
                column = (far_index * 2 + near_index) * 128
                for matrix in range(3):
                    block = source[near_index * 4 + r % 4, matrix].reshape(outer, 1, rows, 128)
                    if matrix < 2:
                        first = matrix * 512 + column
                        inner_ref[:, pl.ds(at, 1), :, first : first + 128] = block
                    else:
                        down_ref[:, pl.ds(at, 1), :, column : column + 128] = block


def place_hidden(own, side, far, corner, base, outer):
    rows = own.shape[2]
    shapes = [(outer, BLOCK, rows // outer, width) for width in (1024, 512)]
    inner, down = call(
        place_hidden_kernel,
        "place_hidden",
        [shaped(shape) for shape in shapes],
        [full(own.shape)] * 4,
        (own, side, far, corner),
        out_specs=[full(shape) for shape in shapes],
        scalars=jnp.reshape(base, (1,)),
        work=cost(0, 4 * 4 * own.size),
    )
    return inner.reshape(BLOCK * rows, 1024), down.reshape(BLOCK * rows, 512)


def deliver_kernel(s_ref, *refs):
    sources, (gate_ref, up_ref, down_ref) = refs[:BLOCK], refs[BLOCK:]
    for k, source in enumerate(sources):
        at = pl.ds(pl.multiple_of((s_ref[0] ^ k) * 128, 128), 128)
        gate_ref[:, at] = source[:, 0:128].astype(F32)
        up_ref[:, at] = source[:, 128:256].astype(F32)
        down_ref[at, :] = source[:, 256:384].astype(F32).T


def deliver(sources, share):
    rows = sources[0].shape[0]
    shapes = [(rows, 1024), (rows, 1024), (1024, rows)]
    return call(
        deliver_kernel,
        "deliver",
        [shaped(shape, F32) for shape in shapes],
        [full((rows, 384))] * BLOCK,
        sources,
        out_specs=[full(shape) for shape in shapes],
        scalars=jnp.reshape(share, (1,)),
        work=cost(0, 6 * rows * 3072),
    )


def turned(values, lane):
    return jnp.where(lane % HEAD < HEAD // 2, pltpu.roll(values, 96, 1), pltpu.roll(values, 32, 1))


def project_kernel(s_ref, *refs):
    sources, quads, (cos_ref, sin_ref) = refs[:10], refs[10:14], refs[14:16]
    q_ref, k_ref, v_ref, kt_ref, vt_ref, h_ref, w_ref, buffer, arrived = refs[16:]
    step = pl.program_id(0)
    base = s_ref[4]
    width = q_ref.shape[1]

    def fetch(slot):
        choices = sources[2 * slot : 2 * slot + 2] if slot < 3 else sources[6:]
        for index, source in enumerate(choices):

            @pl.when(s_ref[5 + slot // 3] == index)
            def _(source=source):
                pltpu.make_async_copy(source, buffer.at[slot % 2], arrived.at[slot % 2]).start()

    @pl.when(step == 0)
    def _():
        fetch(0)
        outer, _, rows, _ = w_ref.shape
        for r in range(BLOCK):
            for part in range(3):
                block = quads[r // 2][r % 2, part].reshape(outer, 1, rows, width)
                w_ref[:, pl.ds(base ^ r, 1), :, part * width : (part + 1) * width] = block

    for slot in range(4):

        @pl.when(step == slot)
        def _(slot=slot):
            if slot < 3:
                fetch(slot + 1)
            here = buffer.at[slot % 2]
            pltpu.make_async_copy(sources[0], here, arrived.at[slot % 2]).wait()
            h_ref[...] = here[...]

    weight = w_ref[...].reshape(h_ref.shape[1], 3 * width)
    raw = dot(h_ref[...], weight, NN)
    cosine, sine = cos_ref[...], sin_ref[...]
    lane = lax.broadcasted_iota(jnp.int32, cosine.shape, 1)
    for target, first in ((q_ref, 0), (k_ref, width)):
        for column in range(0, width, 128):
            tile = raw[:, first + column : first + column + 128]
            turn = tile * cosine + turned(tile, lane) * sine
            target[:, column : column + 128] = turn.astype(BF16)
            if first:
                kt_ref[column : column + 128, :] = turn.T.astype(BF16)
    values = raw[:, 2 * width :]
    v_ref[...] = values.astype(BF16)
    vt_ref[...] = values.T.astype(BF16)


def project(sources, quads, cosine, sine, scalars, outer):
    step, depth = sources[0].shape
    _, _, rows, width = quads[0].shape
    narrow = pl.BlockSpec((step, width), lambda j, s: (s[j], 0))
    tall = pl.BlockSpec((width, step), lambda j, s: (0, s[j]))
    table = pl.BlockSpec((step, 128), lambda j, s: (s[j], 0))
    flat, deep = shaped((WIN, width)), shaped((width, WIN))
    weight = (outer, BLOCK, rows // outer, 3 * width)
    return call(
        project_kernel,
        "project",
        [flat, flat, flat, deep, deep, shaped((WIN, depth)), shaped(weight)],
        [pl.BlockSpec(memory_space=pl.ANY)] * 10 + [held(quads[0].shape)] * 4 + [table, table],
        (*sources, *quads, cosine, sine),
        grid=(4,),
        out_specs=[
            narrow,
            narrow,
            narrow,
            tall,
            tall,
            pl.BlockSpec((step, depth), lambda j, s: (s[j], 0)),
            full(weight),
        ],
        scalars=scalars,
        scratch=[pltpu.VMEM((2, step, depth), BF16), pltpu.SemaphoreType.DMA((2,))],
        work=cost(6 * WIN * depth * width, 6 * WIN * depth),
    )


def attend_kernel(_, q_ref, k_ref, vt_ref, bias_ref, *refs, step):
    *outs, lse_ref = refs
    rows = q_ref.shape[0]
    lane = lax.broadcasted_iota(jnp.int32, (rows, 128), 1)
    query = q_ref[...]
    mixed = []
    for head in range(2):
        own = (lane >= HEAD) == (head == 1)
        masked_query = jnp.where(own, query, jnp.zeros_like(query))
        place_v = slice(HEAD * head, HEAD * head + HEAD)
        top = None
        for first in range(0, WIN, step):
            keys = slice(first, first + step)
            scores = dot(k_ref[keys, :], masked_query, NT) * SCORE_LOG2 + bias_ref[keys, :1]
            block_top = jnp.max(scores, axis=0, keepdims=True)
            new_top = block_top if top is None else jnp.maximum(top, block_top)
            weights = jnp.exp2(scores - new_top)
            part = dot(vt_ref[place_v, keys], weights.astype(BF16), NN)
            part_sum = jnp.sum(weights, axis=0, keepdims=True)
            if top is None:
                sums, total = part, part_sum
            else:
                fade = jnp.exp2(top - new_top)
                sums, total = sums * fade + part, total * fade + part_sum
            top = new_top
        mixed.append(sums * (1.0 / total))
        lse_ref[0, head : head + 1, :] = top + jnp.log2(total)
    result = jnp.concatenate(mixed, axis=0).T.astype(BF16)
    chunk = outs[0].shape[0]
    per = rows // chunk
    for index in range(per):
        outs[index][...] = result[index * chunk : (index + 1) * chunk]


def attend(query, key, value_t, bias, chunk, part, rows=1024, step=512):
    width = query.shape[1]
    pairs = width // 128
    return call(
        functools.partial(attend_kernel, step=step),
        "attend",
        [shaped((chunk, width))] * 2 + [shaped((pairs, 2, rows), F32)],
        [
            pl.BlockSpec((rows, 128), lambda p, s: (part, p)),
            pl.BlockSpec((WIN, 128), lambda p, s: (0, p)),
            pl.BlockSpec((128, WIN), lambda p, s: (p, 0)),
            full((WIN, 128)),
        ],
        (query, key, value_t, bias),
        grid=(pairs,),
        out_specs=[pl.BlockSpec((chunk, 128), lambda p, s: (0, p))] * 2
        + [pl.BlockSpec((1, 2, rows), lambda p, s: (p, 0, 0))],
        work=cost(8 * WIN * WIN * width, 6 * WIN * width, WIN * WIN * width // HEAD // 2),
    )


def choose(refs, index):
    value = refs[0][...]
    for position, ref in enumerate(refs[1:], 1):
        value = jnp.where(index == position, ref[...], value)
    return value


def attend_back_kernel(_, q_ref, k_ref, v_ref, kt_ref, lse_ref, bias_ref, cosq_ref, sinq_ref,
                       cos_ref, sin_ref, *refs, step):
    mixed_refs, grad_refs = refs[:4], refs[4:8]
    dq_ref, dk_ref, dv_ref, dk_sum, dv_sum = refs[8:]
    rows = q_ref.shape[0]
    index = pl.program_id(0)

    @pl.when(index == 0)
    def _():
        dk_sum[...] = jnp.zeros_like(dk_sum)
        dv_sum[...] = jnp.zeros_like(dv_sum)

    lane = lax.broadcasted_iota(jnp.int32, (rows, 128), 1)
    query, grad = q_ref[...], choose(grad_refs, index)
    product = (grad.astype(F32) * choose(mixed_refs, index).astype(F32)).T
    grad_query = []
    for head in range(2):
        own = (lane >= HEAD) == (head == 1)
        masked_query = jnp.where(own, query, jnp.zeros_like(query))
        masked_grad = jnp.where(own, grad, jnp.zeros_like(grad))
        part = slice(HEAD * head, HEAD * head + HEAD)
        row_dot = jnp.sum(product[part, :], axis=0, keepdims=True)
        log_total = lse_ref[0, head : head + 1, :]
        sums = None
        for first in range(0, WIN, step):
            keys = slice(first, first + step)
            scores = dot(k_ref[keys, :], masked_query, NT) * SCORE_LOG2 + bias_ref[keys, :1]
            weights = jnp.exp2(scores - log_total)
            grad_weights = dot(v_ref[keys, :], masked_grad, NT)
            grad_scores = (weights * (grad_weights - row_dot)).astype(BF16)
            dv_sum[keys, :] += dot(weights.astype(BF16), masked_grad, NN)
            dk_sum[keys, :] += dot(grad_scores, masked_query, NN)
            more = dot(kt_ref[part, keys], grad_scores, NN)
            sums = more if sums is None else sums + more
        grad_query.append(sums)

    def unturn(values, cosine, sine):
        at = lax.broadcasted_iota(jnp.int32, values.shape, 1)
        return ((values * cosine - turned(values, at) * sine) * SCALE).astype(BF16)

    dq_ref[...] = unturn(jnp.concatenate(grad_query, axis=0).T, cosq_ref[...], sinq_ref[...])

    @pl.when(index == pl.num_programs(0) - 1)
    def _():
        dk_ref[...] = unturn(dk_sum[...], cos_ref[...], sin_ref[...])
        dv_ref[...] = dv_sum[...].astype(BF16)


def attend_back(pair, query, key, value, key_t, mixed, grad, lse, bias, cosine, sine, step=512):
    rows = grad[0].shape[0]
    block = pl.BlockSpec((rows, 128), lambda i, s: (i, pair))
    piece = pl.BlockSpec((rows, 128), lambda i, s: (0, pair))
    whole = pl.BlockSpec((WIN, 128), lambda i, s: (0, pair))
    local = pl.BlockSpec((rows, 128), lambda i, s: (i, 0))
    return call(
        functools.partial(attend_back_kernel, step=step),
        "attend_back",
        [shaped((WIN, 128))] * 3,
        [
            block,
            whole,
            whole,
            pl.BlockSpec((128, WIN), lambda i, s: (pair, 0)),
            pl.BlockSpec((1, 2, rows), lambda i, s: (pair, 0, i)),
            full((WIN, 128)),
            local,
            local,
            full((WIN, 128)),
            full((WIN, 128)),
        ]
        + [piece] * 8,
        (query, key, value, key_t, lse, bias, cosine, sine, cosine, sine, *mixed, *grad),
        grid=(WIN // rows,),
        out_specs=[local, full((WIN, 128)), full((WIN, 128))],
        scratch=[pltpu.VMEM((WIN, 128), F32)] * 2,
        work=cost(40 * WIN * WIN * 128, 16 * WIN * 128, WIN * WIN * 2),
    )


def unproject_kernel(_, *refs):
    grads, (weight_ref, out_ref) = refs[:-2], refs[-2:]
    grad = jnp.concatenate([ref[...] for ref in grads], axis=1)
    out_ref[...] = dot(grad, weight_ref[...], NT).astype(BF16)


def unproject(grads, weight, scalars, slot):
    depth, triple = weight.shape
    step = WIN // 4
    spec = pl.BlockSpec((step, 128), lambda j, s: (s[slot], 0))
    return call(
        unproject_kernel,
        "unproject",
        shaped((step, depth)),
        [spec] * len(grads) + [full((depth, triple))],
        (*grads, weight),
        out_specs=full((step, depth)),
        scalars=scalars,
        work=cost(2 * step * depth * triple, 4 * step * depth),
    )


def weight_grad_kernel(s_ref, rows_ref, *refs):
    grads, out_ref = refs[:-1], refs[-1]
    grad = jnp.concatenate([ref[...] for ref in grads], axis=1)
    total = dot(rows_ref[...], grad, TN).astype(BF16)
    part = pl.program_id(0)
    rows = out_ref.shape[1]
    count = total.shape[0] // rows
    for index in range(count):
        out_ref[s_ref[4] ^ (part * count + index)] = total[index * rows : (index + 1) * rows]


def weight_grad(rows, grads, scalars):
    depth, triple = rows.shape[1], 128 * len(grads)
    parts = 2
    out = (BLOCK, depth // BLOCK, triple)
    return call(
        weight_grad_kernel,
        "weight_grad",
        shaped(out),
        [pl.BlockSpec((WIN, depth // parts), lambda j, s: (0, j))] + [held((WIN, 128))] * len(grads),
        (rows, *grads),
        grid=(parts,),
        out_specs=full(out),
        scalars=scalars,
        work=cost(2 * WIN * depth * triple, 4 * WIN * depth),
    )


def out_norm_kernel(s_ref, m0, m1, m2, m3, own_ref, other_ref, tokens_ref, gain_ref, bias_ref,
                    residual_ref, normed_ref, weight_ref):
    outer, _, rows, _ = weight_ref.shape
    width = m0.shape[1]

    @pl.when(pl.program_id(0) == 0)
    def _():
        for r in range(BLOCK):
            source = own_ref if r % 2 == 0 else other_ref
            for group in range(4):
                block = source[r // 2, group].reshape(outer, 1, rows, width)
                columns = slice(group * width, (group + 1) * width)
                weight_ref[:, pl.ds(s_ref[0] ^ r, 1), :, columns] = block

    weight = weight_ref[...].reshape(residual_ref.shape[1], 4 * width)
    mixed = jnp.concatenate([ref[...] for ref in (m0, m1, m2, m3)], axis=1)
    residual = tokens_ref[...].astype(F32) + dot(mixed, weight, NT)
    residual_ref[...] = residual
    normed_ref[...] = (unit_of(residual)[0] * gain_ref[...] + bias_ref[...]).astype(BF16)


def out_norm(mixed, own, other, tokens, gain, bias, inner, outer):
    chunk, width = mixed[0].shape
    depth = tokens.shape[1]
    step = chunk // 2
    rows = own.shape[2]
    weight = (outer, BLOCK, rows // outer, 4 * width)
    by_rows = pl.BlockSpec((step, depth), lambda j, s: (j, 0))
    residual, normed, placed = call(
        out_norm_kernel,
        "out_norm",
        [shaped(tokens.shape, F32), shaped(tokens.shape), shaped(weight)],
        [pl.BlockSpec((step, width), lambda j, s: (j, 0))] * 4
        + [held(own.shape)] * 2
        + [by_rows, full((1, depth)), full((1, depth))],
        (*mixed, own, other, tokens, gain[None], bias[None]),
        grid=(2,),
        out_specs=[by_rows, by_rows, full(weight)],
        scalars=jnp.reshape(inner, (1,)),
        work=cost(2 * chunk * depth * depth, 12 * tokens.size),
    )
    return residual, normed, placed.reshape(depth, 4 * width)


def middle_back_kernel(_, own_ref, own2_ref, side_ref, near_ref, corner_ref, cot_ref, residual_ref,
                       gain_ref, weight_ref, grad_ref, low_ref, g0, g1, g2, g3, sums_ref):
    step = pl.program_id(0)
    grad_rows = own_ref[...].astype(F32)
    for ref in (own2_ref, side_ref, near_ref, corner_ref):
        grad_rows = grad_rows + ref[...].astype(F32)
    change, sums = norm_back(grad_rows, residual_ref[...], gain_ref[...])
    grad = cot_ref[...].astype(F32) + change
    grad_ref[...] = grad
    low = grad.astype(BF16)
    low_ref[...] = low
    back = dot(low, weight_ref[...], NN).astype(BF16)
    width = g0.shape[1]
    for k, ref in enumerate((g0, g1, g2, g3)):
        ref[...] = back[:, k * width : (k + 1) * width]

    @pl.when(step == 0)
    def _():
        sums_ref[...] = jnp.zeros_like(sums_ref)

    sums_ref[0:1, :] += sums[0]
    sums_ref[1:2, :] += sums[1]


def middle_back(parts, cotangent, residual, gain, weight):
    rows, depth = cotangent.shape
    width = depth // 4
    step = rows // 2
    by_rows = pl.BlockSpec((step, depth), lambda j, s: (j, 0))
    narrow = pl.BlockSpec((step, width), lambda j, s: (j, 0))
    return call(
        middle_back_kernel,
        "middle_back",
        [shaped((rows, depth), F32), shaped((rows, depth))]
        + [shaped((rows, width))] * 4
        + [shaped((2, depth), F32)],
        [by_rows] * 7 + [full((1, depth)), held(weight.shape)],
        (*parts, cotangent, residual, gain[None], weight),
        grid=(2,),
        out_specs=[by_rows, by_rows] + [narrow] * 4 + [full((2, depth))],
        work=cost(2 * rows * depth * depth, 24 * rows * depth),
    )


def out_grad_kernel(s_ref, low_ref, m0, m1, m2, m3, keep_ref, give_ref):
    mixed = jnp.concatenate([ref[...] for ref in (m0, m1, m2, m3)], axis=1)
    total = dot(low_ref[...], mixed, TN).astype(BF16)
    rows = keep_ref.shape[1]
    for index in range(BLOCK):
        block = total[index * rows : (index + 1) * rows]
        place = s_ref[0] ^ index

        @pl.when(place % 2 == 0)
        def _(block=block, place=place):
            keep_ref[place // 2] = block

        @pl.when(place % 2 == 1)
        def _(block=block, place=place):
            give_ref[place // 2] = block


def out_grad_blocks(low, mixed, inner):
    rows, depth = low.shape
    width = mixed[0].shape[1]
    out = (4, depth // BLOCK, 4 * width)
    return call(
        out_grad_kernel,
        "out_grad",
        [shaped(out)] * 2,
        [full(low.shape)] + [full((rows, width))] * 4,
        (low, *mixed),
        out_specs=[full(out)] * 2,
        scalars=jnp.reshape(inner, (1,)),
        work=cost(2 * rows * depth * depth, 6 * rows * depth),
    )


def first_back_kernel(s_ref, sent_ref, end_ref, own_ref, got_ref, grad_ref, tokens_ref, gain_ref,
                      out_ref, sums_ref):
    own = jnp.where(s_ref[0] == 1, own_ref[...].astype(F32) + got_ref[...].astype(F32), 0.0)
    grad_rows = own + jnp.where(s_ref[1] == 1, end_ref[...], sent_ref[...]).astype(F32)
    change, sums = norm_back(grad_rows, tokens_ref[...].astype(F32), gain_ref[...])
    out_ref[...] = (grad_ref[...] + change).astype(BF16)

    @pl.when(pl.program_id(0) == 0)
    def _():
        sums_ref[...] = jnp.zeros_like(sums_ref)

    sums_ref[0:1, :] += sums[0]
    sums_ref[1:2, :] += sums[1]


def first_back(parts, grad, tokens, gain, flags):
    rows, depth = tokens.shape
    by_rows = pl.BlockSpec((rows // 2, depth), lambda j, s: (j, 0))
    return call(
        first_back_kernel,
        "first_back",
        [shaped(tokens.shape), shaped((2, depth), F32)],
        [by_rows] * 6 + [full((1, depth))],
        (*parts, grad, tokens, gain[None]),
        grid=(2,),
        out_specs=[by_rows, full((2, depth))],
        scalars=flags,
        work=cost(0, 16 * tokens.size),
    )


def hidden_back_kernel(_, a_ref, b_ref, down_ref, out_ref):
    step = pl.program_id(0)
    rows = jnp.where(step == 0, a_ref[...], b_ref[...])
    out_ref[...] = dot(rows, down_ref[...], NN).astype(BF16)


def hidden_back(pair, down):
    rows, depth = pair[0].shape
    hidden = down.shape[1]
    return call(
        hidden_back_kernel,
        "hidden_back",
        shaped((2 * rows, hidden)),
        [full((rows, depth))] * 2 + [held(down.shape)],
        (*pair, down),
        grid=(2,),
        out_specs=pl.BlockSpec((rows, hidden), lambda j, s: (j, 0)),
        work=cost(4 * rows * depth * hidden, 4 * rows * depth),
    )


def feed_kernel(_, a_ref, b_ref, grad_ref, inner_ref, down_ref,
                hidden_ref, both_ref, back_ref, out_ref, other_ref):
    step = pl.program_id(0)
    width = down_ref.shape[1]
    depth = a_ref.shape[1]
    rows = jnp.where(step == 0, a_ref[...], b_ref[...])
    gate = dot(rows, inner_ref[:, :width], NN)
    up = dot(rows, inner_ref[:, width:], NN)
    sigmoid = 1.0 / (1.0 + jnp.exp(-gate))
    activated = gate * sigmoid
    hidden = (activated * up).astype(BF16)
    hidden_ref[...] = hidden
    grad = grad_ref[...].astype(F32)
    grad_gate = (grad * up * sigmoid * (1.0 + gate * (1.0 - sigmoid))).astype(BF16)
    grad_up = (grad * activated).astype(BF16)
    both_ref[:, :width] = grad_gate
    both_ref[:, width:] = grad_up
    back = dot(grad_gate, inner_ref[:, :width], NT) + dot(grad_up, inner_ref[:, width:], NT)
    out = dot(hidden, down_ref[...], NT)

    @pl.when(step == 0)
    def _():
        back_ref[...] = back.astype(BF16)
        out_ref[...] = out.astype(BF16)

    @pl.when(step == 1)
    def _():
        other_ref[:, :depth] = back.astype(BF16)
        other_ref[:, depth:] = out.astype(BF16)


def feed(pair, grad, inner, down):
    rows, depth = pair[0].shape
    hidden = down.shape[1]
    return call(
        feed_kernel,
        "feed",
        [
            shaped((2 * rows, hidden)),
            shaped((2 * rows, 2 * hidden)),
            shaped((rows, depth)),
            shaped((rows, depth)),
            shaped((rows, 2 * depth)),
        ],
        [full((rows, depth))] * 2
        + [pl.BlockSpec((rows, hidden), lambda j, s: (j, 0)), held(inner.shape), held(down.shape)],
        (*pair, grad, inner, down),
        grid=(2,),
        out_specs=[
            pl.BlockSpec((rows, hidden), lambda j, s: (j, 0)),
            pl.BlockSpec((rows, 2 * hidden), lambda j, s: (j, 0)),
            full((rows, depth)),
            full((rows, depth)),
            full((rows, 2 * depth)),
        ],
        work=cost(20 * rows * depth * hidden, 12 * rows * depth),
    )


def hidden_grad_kernel(s_ref, *refs):
    rows, cots, both, hiddens = refs[:8], refs[8:16], refs[16:20], refs[20:24]
    out_ref, total, *buffers, arrived = refs[24:]
    size, half = buffers[0].shape[1:]
    width = hiddens[0].shape[1]
    columns = pl.ds(pl.multiple_of(s_ref[0] * half, half), half)

    def copies(index):
        at = pl.ds(index % 2 * size, size)
        sources = (
            rows[index].at[:, columns],
            cots[index].at[:, columns],
            both[index // 2].at[at, :],
            hiddens[index // 2].at[at, :],
        )
        return [
            pltpu.make_async_copy(source, buffer.at[index % 2], arrived.at[index % 2, number])
            for number, (source, buffer) in enumerate(zip(sources, buffers, strict=True))
        ]

    for copy in copies(0):
        copy.start()
    for index in range(8):
        if index < 7:
            for copy in copies(index + 1):
                copy.start()
        for copy in copies(index):
            copy.wait()
        row, cot, grad, hidden = (buffer[index % 2] for buffer in buffers)
        inner = dot(row, grad, TN)
        down = dot(cot, hidden, TN)
        if index == 0:
            total[:, : 2 * width] = inner
            total[:, 2 * width :] = down
        else:
            total[:, : 2 * width] += inner
            total[:, 2 * width :] += down
    for block in range(half // 128):
        for column in range(4):
            for matrix in range(3):
                first = matrix * width + column * 128
                last = (column * 3 + matrix) * 128
                out_ref[block ^ s_ref[1], :, last : last + 128] = total[
                    block * 128 : (block + 1) * 128, first : first + 128
                ].astype(BF16)


def hidden_grads(rows, cots, both, hiddens, scalars):
    size, depth = rows[0].shape
    width = hiddens[0].shape[1]
    half = depth // 2
    out = (4, 128, 3 * width)
    return call(
        hidden_grad_kernel,
        "hidden_grads",
        shaped(out),
        [pl.BlockSpec(memory_space=pl.ANY)] * 24,
        (*rows, *cots, *both, *hiddens),
        out_specs=full(out),
        scalars=scalars,
        scratch=[
            pltpu.VMEM((half, 3 * width), F32),
            pltpu.VMEM((2, size, half), BF16),
            pltpu.VMEM((2, size, half), BF16),
            pltpu.VMEM((2, size, 2 * width), BF16),
            pltpu.VMEM((2, size, width), BF16),
            pltpu.SemaphoreType.DMA((2, 4)),
        ],
        work=cost(24 * size * depth * width, 20 * size * depth),
    )


def split_kernel(_, a_ref, b_ref, *targets):
    width = targets[0].shape[1]
    for k, target in enumerate(targets):
        block, column = k % 4, slice(k // 4 * width, (k // 4 + 1) * width)
        total = a_ref[block, :, column].astype(F32) + b_ref[block, :, column].astype(F32)
        target[...] = total.astype(BF16)


def split(left, right):
    _, rows, double = left.shape
    out = (rows, double // 2)
    return call(
        split_kernel,
        "split",
        [shaped(out)] * BLOCK,
        [full(left.shape), full(right.shape)],
        (left, right),
        out_specs=[full(out)] * BLOCK,
        work=cost(0, 6 * left.size),
    )


def add(*arrays):
    total = arrays[0].astype(F32)
    for array in arrays[1:]:
        total = total + array.astype(F32)
    return total.astype(BF16)


def after(value, *others):
    return lax.optimization_barrier((value, *others))[0]


def window_moves(rule):
    def target(d, t):
        core, place = rule[d & 1, t]
        return (d & ~1) | core, place

    return target


FIRST = window_moves(
    {
        (0, 0): (1, 0), (0, 1): (0, 0), (0, 2): (0, 1), (0, 3): (0, 2),
        (1, 0): (1, 1), (1, 1): (1, 2), (1, 2): (1, 3), (1, 3): (0, 3),
    }
)
SECOND = window_moves(
    {
        (0, 0): (1, 1), (0, 1): (0, 0), (0, 2): (0, 1), (0, 3): (0, 3),
        (1, 0): (1, 0), (1, 1): (1, 2), (1, 2): (1, 3), (1, 3): (0, 2),
    }
)
THIRD = window_moves(
    {
        (0, 0): (0, 1), (0, 1): (0, 0), (0, 2): (0, 2), (0, 3): (0, 3),
        (1, 0): (1, 0), (1, 1): (1, 1), (1, 2): (1, 3), (1, 3): (1, 2),
    }
)
SECOND_BACK = window_moves(
    {
        (0, 0): (0, 1), (0, 1): (0, 2), (0, 2): (1, 3), (0, 3): (0, 3),
        (1, 0): (1, 0), (1, 1): (0, 0), (1, 2): (1, 1), (1, 3): (1, 2),
    }
)
FIRST_BACK = window_moves(
    {
        (0, 0): (0, 1), (0, 1): (0, 2), (0, 2): (0, 3), (0, 3): (1, 3),
        (1, 0): (0, 0), (1, 1): (1, 0), (1, 2): (1, 1), (1, 3): (1, 2),
    }
)


def collect_window(links, own, tip, early, late):
    first = links.move(own, FIRST)
    second = links.move(after(jnp.where(tip, own, first), *early), SECOND)
    third = links.move(after(second, *late), THIRD)
    sources = []
    for array in (own, first, second, third):
        sources += [array, links.swap(array, CORE)]
    return sources + [sources[5], sources[4]], second, third


def return_window(links, parts, owned, line):
    got = [links.swap(part, CORE) for part in parts[::-1]][::-1]
    inside = (line == 1) | (line == 2)
    zero = jnp.zeros((), BF16)
    last = add(parts[3], got[3])
    third = links.move(last, THIRD)
    outer_end = inside & ~owned
    second = links.move(
        jnp.where(outer_end, last, add(parts[2], got[2], jnp.where(inside, third, zero))), SECOND_BACK
    )
    first = links.move(
        add(
            jnp.where(inside, second, zero),
            jnp.where(owned, parts[1], zero),
            jnp.where(owned, got[1], zero),
        ),
        FIRST_BACK,
    )
    return first, second, parts[0], got[0]


def collect_block(links, rows):
    half = rows.shape[0] // 2
    side, near = links.swap(rows, SIDE), links.swap(rows, NEAR)
    corner = jnp.concatenate(
        [links.swap(near[:half], SIDE), links.swap(side[half:], NEAR)], axis=0
    )
    return rows, side, near, corner


def collect_block_late(links, rows, gate, later):
    side = links.swap(rows, SIDE)
    near = links.swap(after(rows, gate), NEAR)
    corner = links.swap(after(near, later), SIDE)
    return [(part, links.swap(part, CORE)) for part in (rows, side, near, corner)]


def per_device(
    links,
    tokens,
    lengths,
    cotangent,
    attention_gain,
    attention_bias,
    query_weight,
    key_weight,
    value_weight,
    out_weight,
    feedforward_gain,
    feedforward_bias,
    gate_weight,
    up_weight,
    down_weight,
):
    outer = links.outer
    dp = lax.axis_index("dp")
    line = lax.axis_index("tensor")
    core, inner = dp % 2, dp % BLOCK
    side_bit, far_bit = dp // 2 % 2, dp // 4 % 2
    near_bit = line % 2
    window = line // 2
    owned = core == window
    ends = (line == 0) | (line == 3)
    share = near_bit * 2 + core
    hidden_share = near_bit * 4 + side_bit * 2 + core
    width = query_weight.shape[1]
    chunk, depth = tokens.shape

    def by_block(array):
        if outer == 1:
            return array
        shape = (array.shape[0], outer, BLOCK, depth // (outer * BLOCK))
        return array.reshape(shape).transpose(0, 2, 1, 3).reshape(array.shape)

    qkv = links.gather_outer(jnp.stack([query_weight, key_weight, value_weight]), 1)
    pair = jnp.stack(
        [
            links.move(
                qkv, lambda d, t, k=k: ((d & ~1) | (t % 2), t // 2 + 2 * ((d & 1) ^ k))
            )
            for k in range(2)
        ]
    )
    corner_mask = (SIDE[0] | FAR_SIDE[0], 0)
    quads = [pair] + [links.swap(pair, mask) for mask in (SIDE, FAR_SIDE, corner_mask)]

    order_chunk = jnp.arange(4, dtype=jnp.int32) ^ share
    positions = (order_chunk[:, None] * chunk + jnp.arange(chunk, dtype=jnp.int32)).reshape(-1)
    lane = jnp.arange(128, dtype=jnp.int32)
    frequency = jnp.power(ROTARY_BASE, -(lane % (HEAD // 2)).astype(F32) * 2.0 / HEAD)
    angles = positions.astype(F32)[:, None] * frequency[None, :]
    cosine = jnp.cos(angles)
    sine = jnp.sin(angles) * jnp.where(lane % HEAD < HEAD // 2, -1.0, 1.0)

    blocks = pack_hidden(
        links.gather_outer(gate_weight, 0),
        links.gather_outer(up_weight, 0),
        links.gather_outer(down_weight, 1),
        hidden_share,
    )
    mine = jnp.stack(
        [blocks[0]]
        + [
            links.swap(
                blocks[k],
                ((SIDE[0] if k & 2 else 0) | (k & 1), NEAR[1] if k & 4 else 0),
            )
            for k in range(1, BLOCK)
        ]
    )

    normed_first = norm_rows(tokens, attention_gain, attention_bias)
    sources, second_round, last_round = collect_window(
        links, normed_first, owned & ends, (pair, cosine, sine), (*quads, mine)
    )

    piece = after(links.gather_outer(out_weight.T, 0), second_round)
    both_mask = (0, NEAR[1] | FAR[1])
    line_pieces = jnp.stack([piece] + [links.swap(piece, mask) for mask in (NEAR, FAR, both_mask)])
    mine = after(mine, last_round)
    far, far_side = links.swap(mine, FAR), links.swap(mine, FAR_SIDE)
    length = jnp.where(core == window, lengths, links.swap(lengths, CORE))
    bias = jnp.where(positions < length[0], 0.0, MASKED).astype(F32)
    bias = jnp.broadcast_to(bias[:, None], (WIN, 128))
    slot = jnp.arange(4, dtype=jnp.int32)
    slot_chunk = jnp.where(line < 2, line + slot, line - slot) % 4
    last_source = jnp.where(ends, 1 - owned.astype(jnp.int32), 3 - owned.astype(jnp.int32))
    scalars = jnp.concatenate(
        [
            slot_chunk ^ share,
            jnp.stack([(inner // 2) * 2 + window, 1 - owned.astype(jnp.int32), last_source]),
        ]
    ).astype(jnp.int32)

    query, key, value, key_t, value_t, rows_first, weight_qkv = project(
        sources, quads, cosine, sine, scalars, outer
    )
    m0, m1, lse = attend(after(query, mine), key, value_t, bias, chunk, 0)
    cots = collect_block_late(links, after(cotangent, last_round), mine, m0)
    weight_in, weight_down = place_hidden(
        mine, far_side, far, links.swap(after(far, m0), FAR_SIDE), inner, outer
    )
    pieces = after(line_pieces, m0)
    out_own = jnp.stack(
        [pieces] + [links.swap(pieces, mask) for mask in (SIDE, FAR_SIDE, corner_mask)]
    )
    m2, m3, lse_late = attend(after(query, m0, far_side, line_pieces), key, value_t, bias, chunk, 1)
    out_other = links.swap(after(out_own, m2), CORE)
    mixed, lse = (m0, m1, m2, m3), jnp.concatenate([lse, lse_late], axis=2)

    def to_owner(k):
        def rule(d, t):
            return (d & ~1) | (t // 2), ((t % 2) * 2 + (d & 1)) ^ k

        return rule

    def to_heads(k):
        def rule(d, t):
            who = t ^ k
            return (d & ~1) | (who & 1), (who >> 1) + 2 * (d & 1)

        return rule

    attended = [links.move(mixed[k], to_owner(k)) for k in range(4)]
    residual, normed_second, weight_out = out_norm(
        attended, out_own, out_other, after(tokens, far, *cots[1], *cots[2], *cots[3]), feedforward_gain, feedforward_bias, inner, outer
    )

    masks = (SIDE, NEAR, (SIDE[0], NEAR[1]))
    fed, others, totals, gates = [], [], [], ()
    grad_hidden = [hidden_back(cot, weight_down) for cot in cots]
    rows = []
    for q, part in enumerate(collect_block(links, normed_second)):
        rows.append((part, links.swap(part, CORE)))
        own_rows = after(part, *gates)
        fed.append(feed((own_rows, rows[q][1]), grad_hidden[q], weight_in, weight_down))
        others.append(links.swap(fed[q][4], CORE))
        gates = (fed[q][0], *totals[-1:])
        if q:
            totals.append(add(fed[q][2], others[q][:, :depth]))
    back_sent = [links.swap(total, mask) for total, mask in zip(totals, masks, strict=True)]
    hiddens, boths, backs, outs, _ = zip(*fed, strict=True)

    def hidden_half(index, *gates):
        flat = [part for pair_rows in rows for part in pair_rows]
        flat[0] = after(flat[0], *gates)
        flat_cots = [part for cot in cots for part in cot]
        if outer > 1:
            flat = [by_block(part) for part in flat]
            flat_cots = [by_block(part) for part in flat_cots]
        where = jnp.stack([index, side_bit * 2 + core])
        return hidden_grads(flat, flat_cots, boths, hiddens, where)

    hidden_given = hidden_half(1 - far_bit, *totals)
    hidden_got = links.swap(hidden_given, FAR_SIDE)
    out_totals = [add(outs[q], others[q][:, depth:]) for q in (1, 3)]
    grad_residual, grad_attn, *grad_attended, sums_second = middle_back(
        (backs[0], others[0][:, :depth], *back_sent),
        after(cotangent, hidden_given, *out_totals),
        residual,
        feedforward_gain,
        weight_out,
    )
    grad_mixed = [links.move(grad_attended[k], to_heads(k)) for k in range(4)]

    hidden_kept = hidden_half(far_bit, grad_attn)
    out_sent = [links.swap(after(total, *grad_mixed), SIDE) for total in out_totals]
    out_total = add(outs[2], others[2][:, depth:], out_sent[1])
    out_sent[1] = links.swap(out_total, NEAR)
    layer_out = (
        residual
        + outs[0].astype(F32)
        + others[0][:, depth:].astype(F32)
        + out_sent[0].astype(F32)
        + out_sent[1].astype(F32)
    ).astype(BF16)

    sums = add(hidden_kept, hidden_got)
    half = sums.shape[2] // 2
    near_part, far_part = sums[:, :, :half], sums[:, :, half:]
    far_got = links.swap(far_part, FAR)
    grad_mixed[0] = after(grad_mixed[0], near_part)
    terms = (query, key, value, key_t, mixed, grad_mixed, lse, bias, cosine, sine)
    back_first = attend_back(0, *terms)
    parts = split(after(near_part, back_first[0]), far_got)
    back_second = attend_back(1, after(query, parts[0], out_sent[0], out_total), *terms[1:])
    parts = [parts[0]] + [
        links.swap(parts[k], ((SIDE[0] if k & 2 else 0) | (k & 1), NEAR[1] if k & 4 else 0))
        for k in range(1, BLOCK)
    ]
    parts = [links.scatter_outer(part, 0) for part in parts]
    gate_grad, up_grad, down_grad = deliver(parts, hidden_share)

    grads = [part for both in zip(back_first, back_second, strict=True) for part in both]
    weight_qkv = after(
        weight_qkv.reshape(depth, 3 * width), out_sent[1], *parts
    )
    sums = [None] * 4
    for slot in (3, 2, 1, 0):
        sums[slot] = unproject(grads, weight_qkv, scalars, slot)
    kept, given = out_grad_blocks(after(by_block(grad_attn), sums[2]), attended, inner)
    out_wide = add(kept, links.swap(given, CORE))
    out_first = add(
        out_wide[0], *(links.swap(out_wide[q], mask) for q, mask in ((1, SIDE), (2, FAR_SIDE), (3, corner_mask)))
    )
    out_sums = add(
        out_first[:, :width],
        *(
            links.swap(out_first[:, q * width : (q + 1) * width], mask)
            for q, mask in ((1, NEAR), (2, FAR), (3, both_mask))
        ),
    )
    out_grad = links.scatter_outer(out_sums, 0).astype(F32).T

    blocks = weight_grad(after(by_block(rows_first), sums[2]), grads, scalars)
    blocks = blocks.reshape(4, 2 * (depth // BLOCK), 3 * width)
    wide = add(
        blocks[0],
        *(links.swap(blocks[q], mask) for q, mask in ((1, SIDE), (2, FAR_SIDE), (3, corner_mask))),
    )
    rows_each = depth // BLOCK
    halves = [
        links.move(
            wide[k * rows_each : (k + 1) * rows_each],
            lambda d, t, k=k: ((d & ~1) | ((t // 2) ^ k), (t % 2) * 2 + (d & 1)),
        )
        for k in range(2)
    ]
    tokens_grad, sums_first = first_back(
        return_window(links, sums, owned, line),
        grad_residual,
        after(tokens, *halves, out_sums),
        attention_gain,
        jnp.stack([owned, owned & ends]),
    )

    sums = links.scatter_outer(add(*halves), 0).astype(F32)

    norms = jnp.concatenate([sums_first, sums_second], axis=0)
    side, far, corner = (links.swap(norms, mask) for mask in (SIDE, FAR_SIDE, corner_mask))
    norms = (norms + side) + (far + corner)
    near, far, both = (links.swap(norms, mask) for mask in (NEAR, FAR, both_mask))
    norms = (norms + near) + (far + both)
    norms = norms + links.swap(norms, CORE)
    for bit in range(3, links.nd.bit_length() - 1):
        norms = norms + links.swap(norms, (1 << bit, 0))
    return (
        layer_out,
        tokens_grad,
        norms[0],
        norms[1],
        sums[:, :width],
        sums[:, width : 2 * width],
        sums[:, 2 * width :],
        out_grad,
        norms[2],
        norms[3],
        gate_grad,
        up_grad,
        down_grad,
    )


def solution(mesh):
    rows, columns = P("dp", "tensor"), P("tensor", "dp")
    spread = P(("dp", "tensor"), None)
    placed = (
        spread, P("dp"), spread, P(), P(), rows, rows, rows, columns, P(), P(), rows, rows, columns
    )
    given = (
        spread, spread, P(), P(), rows, rows, rows, columns, P(), P(), rows, rows, columns
    )
    return jax.shard_map(
        functools.partial(per_device, Links(mesh)),
        mesh=mesh,
        in_specs=placed,
        out_specs=given,
        check_vma=False,
    )
```

```python
import functools
import math

import jax
import jax.numpy as jnp
from jax import lax
from jax.experimental import pallas as pl
from jax.experimental.pallas import tpu as pltpu
from jax.sharding import PartitionSpec as P

HEAD = 64
WIN = 2048
EPSILON = 1e-05
MASKED = -1000000000.0
ROTARY_BASE = 10000.0
SCALE = 1.0 / math.sqrt(HEAD)
SCORE_LOG2 = SCALE * math.log2(math.e)

BLOCK = 8
CORE = (1, 0)
SIDE = (2, 0)
FAR_SIDE = (4, 0)
NEAR = (0, 1)
FAR = (0, 2)

F32 = jnp.float32
BF16 = jnp.bfloat16
NT = (((1,), (1,)), ((), ()))
NN = (((1,), (0,)), ((), ()))
TN = (((0,), (0,)), ((), ()))
VMEM_BYTES = 56 * 1024 * 1024


def dot(left, right, dims):
    return lax.dot_general(left, right, dims, preferred_element_type=F32)


def pick(array, index, axis):
    return lax.dynamic_index_in_dim(array, index, axis, keepdims=False)


class Links:
    def __init__(self, mesh):
        self.nd = mesh.shape["dp"]
        self.nt = mesh.shape["tensor"]
        self.outer = self.nd // BLOCK
        self.groups = [[o * BLOCK + i for o in range(self.outer)] for i in range(BLOCK)]

    def move(self, array, rule):
        pairs = []
        for d in range(self.nd):
            for t in range(self.nt):
                target = rule(d, t)
                if target is not None:
                    pairs.append((d * self.nt + t, target[0] * self.nt + target[1]))
        return lax.ppermute(array, ("dp", "tensor"), pairs)

    def swap(self, array, mask):
        return self.move(array, lambda d, t: (d ^ mask[0], t ^ mask[1]))

    def gather_outer(self, array, axis):
        if self.outer == 1:
            return array
        return lax.all_gather(array, "dp", axis=axis, tiled=True, axis_index_groups=self.groups)

    def scatter_outer(self, array, axis):
        if self.outer == 1:
            return array
        return lax.psum_scatter(
            array, "dp", scatter_dimension=axis, tiled=True, axis_index_groups=self.groups
        )


COST = 3


def cost(flops, moved, exps=0):
    return pl.CostEstimate(
        flops=int(COST * flops), bytes_accessed=int(COST * moved), transcendentals=int(COST * exps)
    )


def params():
    return pltpu.CompilerParams(vmem_limit_bytes=VMEM_BYTES)


def call(kernel, name, outs, ins, operands, *, grid=(1,), out_specs, scalars=None, scratch=(), work=None):
    if scalars is None:
        scalars = jnp.zeros((1,), jnp.int32)
    return pl.pallas_call(
        kernel,
        grid_spec=pltpu.PrefetchScalarGridSpec(
            num_scalar_prefetch=1, grid=grid, in_specs=ins, out_specs=out_specs, scratch_shapes=scratch
        ),
        out_shape=outs,
        compiler_params=params(),
        cost_estimate=work,
        name=name,
    )(scalars.astype(jnp.int32), *operands)


def full(shape):
    return pl.BlockSpec(shape, lambda *_: (0,) * len(shape))


def held(shape):
    return pl.BlockSpec(shape, lambda *_: (0,) * len(shape), pipeline_mode=pl.Buffered(1))


def shaped(shape, kind=BF16):
    return jax.ShapeDtypeStruct(shape, kind)


def unit_of(rows):
    centered = rows - jnp.mean(rows, axis=1, keepdims=True)
    inverse = lax.rsqrt(jnp.mean(centered * centered, axis=1, keepdims=True) + EPSILON)
    return centered * inverse, inverse


def norm_back(grad_rows, rows, scaling):
    unit, inverse = unit_of(rows)
    grad_unit = grad_rows * scaling
    centered = grad_unit - jnp.mean(grad_unit, axis=1, keepdims=True)
    slope = jnp.mean(grad_unit * unit, axis=1, keepdims=True)
    sums = (
        jnp.sum(grad_rows * unit, axis=0, keepdims=True),
        jnp.sum(grad_rows, axis=0, keepdims=True),
    )
    return inverse * (centered - unit * slope), sums


def norm_kernel(_, tokens_ref, gain_ref, bias_ref, out_ref):
    rows = tokens_ref[...].astype(F32)
    out_ref[...] = (unit_of(rows)[0] * gain_ref[...] + bias_ref[...]).astype(BF16)


def norm_rows(tokens, gain, bias):
    depth = tokens.shape[1]
    return call(
        norm_kernel,
        "norm_rows",
        shaped(tokens.shape),
        [full(tokens.shape), full((1, depth)), full((1, depth))],
        (tokens, gain[None], bias[None]),
        out_specs=full(tokens.shape),
        work=cost(0, 4 * tokens.size),
    )


def pack_kernel(s_ref, gate_ref, up_ref, down_ref, *targets):
    for k, target in enumerate(targets):
        at = pl.ds(pl.multiple_of((s_ref[0] ^ k) * 128, 128), 128)
        target[0] = gate_ref[:, at]
        target[1] = up_ref[:, at]
        target[2] = down_ref[at, :].astype(F32).T.astype(BF16)


def pack_hidden(gate, up, down, share):
    rows = gate.shape[0]
    block = (3, rows, 128)
    return call(
        pack_kernel,
        "pack_hidden",
        [shaped(block)] * BLOCK,
        [full(gate.shape), full(up.shape), full(down.shape)],
        (gate, up, down),
        out_specs=[full(block)] * BLOCK,
        scalars=jnp.reshape(share, (1,)),
        work=cost(0, 4 * 3 * gate.size),
    )


def place_hidden_kernel(s_ref, own, side, far, corner, inner_ref, down_ref):
    outer, _, rows, _ = inner_ref.shape
    for r in range(BLOCK):
        at = s_ref[0] ^ r
        for far_index, source in enumerate((own, far) if r < 4 else (side, corner)):
            for near_index in range(2):
                column = (far_index * 2 + near_index) * 128
                for matrix in range(3):
                    block = source[near_index * 4 + r % 4, matrix].reshape(outer, 1, rows, 128)
                    if matrix < 2:
                        first = matrix * 512 + column
                        inner_ref[:, pl.ds(at, 1), :, first : first + 128] = block
                    else:
                        down_ref[:, pl.ds(at, 1), :, column : column + 128] = block


def place_hidden(own, side, far, corner, base, outer):
    rows = own.shape[2]
    shapes = [(outer, BLOCK, rows // outer, width) for width in (1024, 512)]
    inner, down = call(
        place_hidden_kernel,
        "place_hidden",
        [shaped(shape) for shape in shapes],
        [full(own.shape)] * 4,
        (own, side, far, corner),
        out_specs=[full(shape) for shape in shapes],
        scalars=jnp.reshape(base, (1,)),
        work=cost(0, 4 * 4 * own.size),
    )
    return inner.reshape(BLOCK * rows, 1024), down.reshape(BLOCK * rows, 512)


def deliver_kernel(s_ref, *refs):
    sources, (gate_ref, up_ref, down_ref) = refs[:BLOCK], refs[BLOCK:]
    for k, source in enumerate(sources):
        at = pl.ds(pl.multiple_of((s_ref[0] ^ k) * 128, 128), 128)
        gate_ref[:, at] = source[:, 0:128].astype(F32)
        up_ref[:, at] = source[:, 128:256].astype(F32)
        down_ref[at, :] = source[:, 256:384].astype(F32).T


def deliver(sources, share):
    rows = sources[0].shape[0]
    shapes = [(rows, 1024), (rows, 1024), (1024, rows)]
    return call(
        deliver_kernel,
        "deliver",
        [shaped(shape, F32) for shape in shapes],
        [full((rows, 384))] * BLOCK,
        sources,
        out_specs=[full(shape) for shape in shapes],
        scalars=jnp.reshape(share, (1,)),
        work=cost(0, 6 * rows * 3072),
    )


def turned(values, lane):
    return jnp.where(lane % HEAD < HEAD // 2, pltpu.roll(values, 96, 1), pltpu.roll(values, 32, 1))


def project_kernel(s_ref, *refs):
    sources, quads, (cos_ref, sin_ref) = refs[:10], refs[10:14], refs[14:16]
    q_ref, k_ref, v_ref, kt_ref, vt_ref, h_ref, w_ref, buffer, arrived = refs[16:]
    step = pl.program_id(0)
    base = s_ref[4]
    width = q_ref.shape[1]

    def fetch(slot):
        choices = sources[2 * slot : 2 * slot + 2] if slot < 3 else sources[6:]
        for index, source in enumerate(choices):

            @pl.when(s_ref[5 + slot // 3] == index)
            def _(source=source):
                pltpu.make_async_copy(source, buffer.at[slot % 2], arrived.at[slot % 2]).start()

    @pl.when(step == 0)
    def _():
        fetch(0)
        outer, _, rows, _ = w_ref.shape
        for r in range(BLOCK):
            for part in range(3):
                block = quads[r // 2][r % 2, part].reshape(outer, 1, rows, width)
                w_ref[:, pl.ds(base ^ r, 1), :, part * width : (part + 1) * width] = block

    for slot in range(4):

        @pl.when(step == slot)
        def _(slot=slot):
            if slot < 3:
                fetch(slot + 1)
            here = buffer.at[slot % 2]
            pltpu.make_async_copy(sources[0], here, arrived.at[slot % 2]).wait()
            h_ref[...] = here[...]

    weight = w_ref[...].reshape(h_ref.shape[1], 3 * width)
    raw = dot(h_ref[...], weight, NN)
    cosine, sine = cos_ref[...], sin_ref[...]
    lane = lax.broadcasted_iota(jnp.int32, cosine.shape, 1)
    for target, first in ((q_ref, 0), (k_ref, width)):
        for column in range(0, width, 128):
            tile = raw[:, first + column : first + column + 128]
            turn = tile * cosine + turned(tile, lane) * sine
            target[:, column : column + 128] = turn.astype(BF16)
            if first:
                kt_ref[column : column + 128, :] = turn.T.astype(BF16)
    values = raw[:, 2 * width :]
    v_ref[...] = values.astype(BF16)
    vt_ref[...] = values.T.astype(BF16)


def project(sources, quads, cosine, sine, scalars, outer):
    step, depth = sources[0].shape
    _, _, rows, width = quads[0].shape
    narrow = pl.BlockSpec((step, width), lambda j, s: (s[j], 0))
    tall = pl.BlockSpec((width, step), lambda j, s: (0, s[j]))
    table = pl.BlockSpec((step, 128), lambda j, s: (s[j], 0))
    flat, deep = shaped((WIN, width)), shaped((width, WIN))
    weight = (outer, BLOCK, rows // outer, 3 * width)
    return call(
        project_kernel,
        "project",
        [flat, flat, flat, deep, deep, shaped((WIN, depth)), shaped(weight)],
        [pl.BlockSpec(memory_space=pl.ANY)] * 10 + [held(quads[0].shape)] * 4 + [table, table],
        (*sources, *quads, cosine, sine),
        grid=(4,),
        out_specs=[
            narrow,
            narrow,
            narrow,
            tall,
            tall,
            pl.BlockSpec((step, depth), lambda j, s: (s[j], 0)),
            full(weight),
        ],
        scalars=scalars,
        scratch=[pltpu.VMEM((2, step, depth), BF16), pltpu.SemaphoreType.DMA((2,))],
        work=cost(6 * WIN * depth * width, 6 * WIN * depth),
    )


def attend_kernel(_, q_ref, k_ref, vt_ref, bias_ref, *refs, step):
    *outs, lse_ref = refs
    rows = q_ref.shape[0]
    lane = lax.broadcasted_iota(jnp.int32, (rows, 128), 1)
    query = q_ref[...]
    mixed = []
    for head in range(2):
        own = (lane >= HEAD) == (head == 1)
        masked_query = jnp.where(own, query, jnp.zeros_like(query))
        place_v = slice(HEAD * head, HEAD * head + HEAD)
        top = None
        for first in range(0, WIN, step):
            keys = slice(first, first + step)
            scores = dot(k_ref[keys, :], masked_query, NT) * SCORE_LOG2 + bias_ref[keys, :1]
            block_top = jnp.max(scores, axis=0, keepdims=True)
            new_top = block_top if top is None else jnp.maximum(top, block_top)
            weights = jnp.exp2(scores - new_top)
            part = dot(vt_ref[place_v, keys], weights.astype(BF16), NN)
            part_sum = jnp.sum(weights, axis=0, keepdims=True)
            if top is None:
                sums, total = part, part_sum
            else:
                fade = jnp.exp2(top - new_top)
                sums, total = sums * fade + part, total * fade + part_sum
            top = new_top
        mixed.append(sums * (1.0 / total))
        lse_ref[0, head : head + 1, :] = top + jnp.log2(total)
    result = jnp.concatenate(mixed, axis=0).T.astype(BF16)
    chunk = outs[0].shape[0]
    per = rows // chunk
    for index in range(per):
        outs[index][...] = result[index * chunk : (index + 1) * chunk]


def attend(query, key, value_t, bias, chunk, part, rows=1024, step=512):
    width = query.shape[1]
    pairs = width // 128
    return call(
        functools.partial(attend_kernel, step=step),
        "attend",
        [shaped((chunk, width))] * 2 + [shaped((pairs, 2, rows), F32)],
        [
            pl.BlockSpec((rows, 128), lambda p, s: (part, p)),
            pl.BlockSpec((WIN, 128), lambda p, s: (0, p)),
            pl.BlockSpec((128, WIN), lambda p, s: (p, 0)),
            full((WIN, 128)),
        ],
        (query, key, value_t, bias),
        grid=(pairs,),
        out_specs=[pl.BlockSpec((chunk, 128), lambda p, s: (0, p))] * 2
        + [pl.BlockSpec((1, 2, rows), lambda p, s: (p, 0, 0))],
        work=cost(8 * WIN * WIN * width, 6 * WIN * width, WIN * WIN * width // HEAD // 2),
    )


def choose(refs, index):
    value = refs[0][...]
    for position, ref in enumerate(refs[1:], 1):
        value = jnp.where(index == position, ref[...], value)
    return value


def attend_back_kernel(_, q_ref, k_ref, v_ref, kt_ref, lse_ref, bias_ref, cosq_ref, sinq_ref,
                       cos_ref, sin_ref, *refs, step):
    mixed_refs, grad_refs = refs[:4], refs[4:8]
    dq_ref, dk_ref, dv_ref, dk_sum, dv_sum = refs[8:]
    rows = q_ref.shape[0]
    index = pl.program_id(0)

    @pl.when(index == 0)
    def _():
        dk_sum[...] = jnp.zeros_like(dk_sum)
        dv_sum[...] = jnp.zeros_like(dv_sum)

    lane = lax.broadcasted_iota(jnp.int32, (rows, 128), 1)
    query, grad = q_ref[...], choose(grad_refs, index)
    product = (grad.astype(F32) * choose(mixed_refs, index).astype(F32)).T
    grad_query = []
    for head in range(2):
        own = (lane >= HEAD) == (head == 1)
        masked_query = jnp.where(own, query, jnp.zeros_like(query))
        masked_grad = jnp.where(own, grad, jnp.zeros_like(grad))
        part = slice(HEAD * head, HEAD * head + HEAD)
        row_dot = jnp.sum(product[part, :], axis=0, keepdims=True)
        log_total = lse_ref[0, head : head + 1, :]
        sums = None
        for first in range(0, WIN, step):
            keys = slice(first, first + step)
            scores = dot(k_ref[keys, :], masked_query, NT) * SCORE_LOG2 + bias_ref[keys, :1]
            weights = jnp.exp2(scores - log_total)
            grad_weights = dot(v_ref[keys, :], masked_grad, NT)
            grad_scores = (weights * (grad_weights - row_dot)).astype(BF16)
            dv_sum[keys, :] += dot(weights.astype(BF16), masked_grad, NN)
            dk_sum[keys, :] += dot(grad_scores, masked_query, NN)
            more = dot(kt_ref[part, keys], grad_scores, NN)
            sums = more if sums is None else sums + more
        grad_query.append(sums)

    def unturn(values, cosine, sine):
        at = lax.broadcasted_iota(jnp.int32, values.shape, 1)
        return ((values * cosine - turned(values, at) * sine) * SCALE).astype(BF16)

    dq_ref[...] = unturn(jnp.concatenate(grad_query, axis=0).T, cosq_ref[...], sinq_ref[...])

    @pl.when(index == pl.num_programs(0) - 1)
    def _():
        dk_ref[...] = unturn(dk_sum[...], cos_ref[...], sin_ref[...])
        dv_ref[...] = dv_sum[...].astype(BF16)


def attend_back(pair, query, key, value, key_t, mixed, grad, lse, bias, cosine, sine, step=512):
    rows = grad[0].shape[0]
    block = pl.BlockSpec((rows, 128), lambda i, s: (i, pair))
    piece = pl.BlockSpec((rows, 128), lambda i, s: (0, pair))
    whole = pl.BlockSpec((WIN, 128), lambda i, s: (0, pair))
    local = pl.BlockSpec((rows, 128), lambda i, s: (i, 0))
    return call(
        functools.partial(attend_back_kernel, step=step),
        "attend_back",
        [shaped((WIN, 128))] * 3,
        [
            block,
            whole,
            whole,
            pl.BlockSpec((128, WIN), lambda i, s: (pair, 0)),
            pl.BlockSpec((1, 2, rows), lambda i, s: (pair, 0, i)),
            full((WIN, 128)),
            local,
            local,
            full((WIN, 128)),
            full((WIN, 128)),
        ]
        + [piece] * 8,
        (query, key, value, key_t, lse, bias, cosine, sine, cosine, sine, *mixed, *grad),
        grid=(WIN // rows,),
        out_specs=[local, full((WIN, 128)), full((WIN, 128))],
        scratch=[pltpu.VMEM((WIN, 128), F32)] * 2,
        work=cost(40 * WIN * WIN * 128, 16 * WIN * 128, WIN * WIN * 2),
    )


def unproject_kernel(_, *refs):
    grads, (weight_ref, out_ref) = refs[:-2], refs[-2:]
    grad = jnp.concatenate([ref[...] for ref in grads], axis=1)
    out_ref[...] = dot(grad, weight_ref[...], NT).astype(BF16)


def unproject(grads, weight, scalars, slot):
    depth, triple = weight.shape
    step = WIN // 4
    spec = pl.BlockSpec((step, 128), lambda j, s: (s[slot], 0))
    return call(
        unproject_kernel,
        "unproject",
        shaped((step, depth)),
        [spec] * len(grads) + [full((depth, triple))],
        (*grads, weight),
        out_specs=full((step, depth)),
        scalars=scalars,
        work=cost(2 * step * depth * triple, 4 * step * depth),
    )


def weight_grad_kernel(s_ref, rows_ref, *refs):
    grads, out_ref = refs[:-1], refs[-1]
    grad = jnp.concatenate([ref[...] for ref in grads], axis=1)
    total = dot(rows_ref[...], grad, TN).astype(BF16)
    part = pl.program_id(0)
    rows = out_ref.shape[1]
    count = total.shape[0] // rows
    for index in range(count):
        out_ref[s_ref[4] ^ (part * count + index)] = total[index * rows : (index + 1) * rows]


def weight_grad(rows, grads, scalars):
    depth, triple = rows.shape[1], 128 * len(grads)
    parts = 2
    out = (BLOCK, depth // BLOCK, triple)
    return call(
        weight_grad_kernel,
        "weight_grad",
        shaped(out),
        [pl.BlockSpec((WIN, depth // parts), lambda j, s: (0, j))] + [held((WIN, 128))] * len(grads),
        (rows, *grads),
        grid=(parts,),
        out_specs=full(out),
        scalars=scalars,
        work=cost(2 * WIN * depth * triple, 4 * WIN * depth),
    )


def out_norm_kernel(s_ref, m0, m1, m2, m3, own_ref, other_ref, tokens_ref, gain_ref, bias_ref,
                    residual_ref, normed_ref, weight_ref):
    outer, _, rows, _ = weight_ref.shape
    width = m0.shape[1]

    @pl.when(pl.program_id(0) == 0)
    def _():
        for r in range(BLOCK):
            source = own_ref if r % 2 == 0 else other_ref
            for group in range(4):
                block = source[r // 2, group].reshape(outer, 1, rows, width)
                columns = slice(group * width, (group + 1) * width)
                weight_ref[:, pl.ds(s_ref[0] ^ r, 1), :, columns] = block

    weight = weight_ref[...].reshape(residual_ref.shape[1], 4 * width)
    mixed = jnp.concatenate([ref[...] for ref in (m0, m1, m2, m3)], axis=1)
    residual = tokens_ref[...].astype(F32) + dot(mixed, weight, NT)
    residual_ref[...] = residual
    normed_ref[...] = (unit_of(residual)[0] * gain_ref[...] + bias_ref[...]).astype(BF16)


def out_norm(mixed, own, other, tokens, gain, bias, inner, outer):
    chunk, width = mixed[0].shape
    depth = tokens.shape[1]
    step = chunk // 2
    rows = own.shape[2]
    weight = (outer, BLOCK, rows // outer, 4 * width)
    by_rows = pl.BlockSpec((step, depth), lambda j, s: (j, 0))
    residual, normed, placed = call(
        out_norm_kernel,
        "out_norm",
        [shaped(tokens.shape, F32), shaped(tokens.shape), shaped(weight)],
        [pl.BlockSpec((step, width), lambda j, s: (j, 0))] * 4
        + [held(own.shape)] * 2
        + [by_rows, full((1, depth)), full((1, depth))],
        (*mixed, own, other, tokens, gain[None], bias[None]),
        grid=(2,),
        out_specs=[by_rows, by_rows, full(weight)],
        scalars=jnp.reshape(inner, (1,)),
        work=cost(2 * chunk * depth * depth, 12 * tokens.size),
    )
    return residual, normed, placed.reshape(depth, 4 * width)


def middle_back_kernel(_, own_ref, own2_ref, side_ref, near_ref, corner_ref, cot_ref, residual_ref,
                       gain_ref, weight_ref, grad_ref, low_ref, g0, g1, g2, g3, sums_ref):
    step = pl.program_id(0)
    grad_rows = own_ref[...].astype(F32)
    for ref in (own2_ref, side_ref, near_ref, corner_ref):
        grad_rows = grad_rows + ref[...].astype(F32)
    change, sums = norm_back(grad_rows, residual_ref[...], gain_ref[...])
    grad = cot_ref[...].astype(F32) + change
    grad_ref[...] = grad
    low = grad.astype(BF16)
    low_ref[...] = low
    back = dot(low, weight_ref[...], NN).astype(BF16)
    width = g0.shape[1]
    for k, ref in enumerate((g0, g1, g2, g3)):
        ref[...] = back[:, k * width : (k + 1) * width]

    @pl.when(step == 0)
    def _():
        sums_ref[...] = jnp.zeros_like(sums_ref)

    sums_ref[0:1, :] += sums[0]
    sums_ref[1:2, :] += sums[1]


def middle_back(parts, cotangent, residual, gain, weight):
    rows, depth = cotangent.shape
    width = depth // 4
    step = rows // 2
    by_rows = pl.BlockSpec((step, depth), lambda j, s: (j, 0))
    narrow = pl.BlockSpec((step, width), lambda j, s: (j, 0))
    return call(
        middle_back_kernel,
        "middle_back",
        [shaped((rows, depth), F32), shaped((rows, depth))]
        + [shaped((rows, width))] * 4
        + [shaped((2, depth), F32)],
        [by_rows] * 7 + [full((1, depth)), held(weight.shape)],
        (*parts, cotangent, residual, gain[None], weight),
        grid=(2,),
        out_specs=[by_rows, by_rows] + [narrow] * 4 + [full((2, depth))],
        work=cost(2 * rows * depth * depth, 24 * rows * depth),
    )


def out_grad_kernel(s_ref, low_ref, m0, m1, m2, m3, keep_ref, give_ref):
    mixed = jnp.concatenate([ref[...] for ref in (m0, m1, m2, m3)], axis=1)
    total = dot(low_ref[...], mixed, TN).astype(BF16)
    rows = keep_ref.shape[1]
    for index in range(BLOCK):
        block = total[index * rows : (index + 1) * rows]
        place = s_ref[0] ^ index

        @pl.when(place % 2 == 0)
        def _(block=block, place=place):
            keep_ref[place // 2] = block

        @pl.when(place % 2 == 1)
        def _(block=block, place=place):
            give_ref[place // 2] = block


def out_grad_blocks(low, mixed, inner):
    rows, depth = low.shape
    width = mixed[0].shape[1]
    out = (4, depth // BLOCK, 4 * width)
    return call(
        out_grad_kernel,
        "out_grad",
        [shaped(out)] * 2,
        [full(low.shape)] + [full((rows, width))] * 4,
        (low, *mixed),
        out_specs=[full(out)] * 2,
        scalars=jnp.reshape(inner, (1,)),
        work=cost(2 * rows * depth * depth, 6 * rows * depth),
    )


def first_back_kernel(s_ref, sent_ref, end_ref, own_ref, got_ref, grad_ref, tokens_ref, gain_ref,
                      out_ref, sums_ref):
    own = jnp.where(s_ref[0] == 1, own_ref[...].astype(F32) + got_ref[...].astype(F32), 0.0)
    grad_rows = own + jnp.where(s_ref[1] == 1, end_ref[...], sent_ref[...]).astype(F32)
    change, sums = norm_back(grad_rows, tokens_ref[...].astype(F32), gain_ref[...])
    out_ref[...] = (grad_ref[...] + change).astype(BF16)

    @pl.when(pl.program_id(0) == 0)
    def _():
        sums_ref[...] = jnp.zeros_like(sums_ref)

    sums_ref[0:1, :] += sums[0]
    sums_ref[1:2, :] += sums[1]


def first_back(parts, grad, tokens, gain, flags):
    rows, depth = tokens.shape
    by_rows = pl.BlockSpec((rows // 2, depth), lambda j, s: (j, 0))
    return call(
        first_back_kernel,
        "first_back",
        [shaped(tokens.shape), shaped((2, depth), F32)],
        [by_rows] * 6 + [full((1, depth))],
        (*parts, grad, tokens, gain[None]),
        grid=(2,),
        out_specs=[by_rows, full((2, depth))],
        scalars=flags,
        work=cost(0, 16 * tokens.size),
    )


def hidden_back_kernel(_, a_ref, b_ref, down_ref, out_ref):
    step = pl.program_id(0)
    rows = jnp.where(step == 0, a_ref[...], b_ref[...])
    out_ref[...] = dot(rows, down_ref[...], NN).astype(BF16)


def hidden_back(pair, down):
    rows, depth = pair[0].shape
    hidden = down.shape[1]
    return call(
        hidden_back_kernel,
        "hidden_back",
        shaped((2 * rows, hidden)),
        [full((rows, depth))] * 2 + [held(down.shape)],
        (*pair, down),
        grid=(2,),
        out_specs=pl.BlockSpec((rows, hidden), lambda j, s: (j, 0)),
        work=cost(4 * rows * depth * hidden, 4 * rows * depth),
    )


def feed_kernel(_, a_ref, b_ref, grad_ref, inner_ref, down_ref,
                hidden_ref, both_ref, back_ref, out_ref, other_ref):
    step = pl.program_id(0)
    width = down_ref.shape[1]
    depth = a_ref.shape[1]
    rows = jnp.where(step == 0, a_ref[...], b_ref[...])
    gate = dot(rows, inner_ref[:, :width], NN)
    up = dot(rows, inner_ref[:, width:], NN)
    sigmoid = 1.0 / (1.0 + jnp.exp(-gate))
    activated = gate * sigmoid
    hidden = (activated * up).astype(BF16)
    hidden_ref[...] = hidden
    grad = grad_ref[...].astype(F32)
    grad_gate = (grad * up * sigmoid * (1.0 + gate * (1.0 - sigmoid))).astype(BF16)
    grad_up = (grad * activated).astype(BF16)
    both_ref[:, :width] = grad_gate
    both_ref[:, width:] = grad_up
    back = dot(grad_gate, inner_ref[:, :width], NT) + dot(grad_up, inner_ref[:, width:], NT)
    out = dot(hidden, down_ref[...], NT)

    @pl.when(step == 0)
    def _():
        back_ref[...] = back.astype(BF16)
        out_ref[...] = out.astype(BF16)

    @pl.when(step == 1)
    def _():
        other_ref[:, :depth] = back.astype(BF16)
        other_ref[:, depth:] = out.astype(BF16)


def feed(pair, grad, inner, down):
    rows, depth = pair[0].shape
    hidden = down.shape[1]
    return call(
        feed_kernel,
        "feed",
        [
            shaped((2 * rows, hidden)),
            shaped((2 * rows, 2 * hidden)),
            shaped((rows, depth)),
            shaped((rows, depth)),
            shaped((rows, 2 * depth)),
        ],
        [full((rows, depth))] * 2
        + [pl.BlockSpec((rows, hidden), lambda j, s: (j, 0)), held(inner.shape), held(down.shape)],
        (*pair, grad, inner, down),
        grid=(2,),
        out_specs=[
            pl.BlockSpec((rows, hidden), lambda j, s: (j, 0)),
            pl.BlockSpec((rows, 2 * hidden), lambda j, s: (j, 0)),
            full((rows, depth)),
            full((rows, depth)),
            full((rows, 2 * depth)),
        ],
        work=cost(20 * rows * depth * hidden, 12 * rows * depth),
    )


def hidden_grad_kernel(s_ref, *refs):
    rows, cots, both, hiddens = refs[:8], refs[8:16], refs[16:20], refs[20:24]
    out_ref, total, *buffers, arrived = refs[24:]
    size, half = buffers[0].shape[1:]
    width = hiddens[0].shape[1]
    columns = pl.ds(pl.multiple_of(s_ref[0] * half, half), half)

    def copies(index):
        at = pl.ds(index % 2 * size, size)
        sources = (
            rows[index].at[:, columns],
            cots[index].at[:, columns],
            both[index // 2].at[at, :],
            hiddens[index // 2].at[at, :],
        )
        return [
            pltpu.make_async_copy(source, buffer.at[index % 2], arrived.at[index % 2, number])
            for number, (source, buffer) in enumerate(zip(sources, buffers, strict=True))
        ]

    for copy in copies(0):
        copy.start()
    for index in range(8):
        if index < 7:
            for copy in copies(index + 1):
                copy.start()
        for copy in copies(index):
            copy.wait()
        row, cot, grad, hidden = (buffer[index % 2] for buffer in buffers)
        inner = dot(row, grad, TN)
        down = dot(cot, hidden, TN)
        if index == 0:
            total[:, : 2 * width] = inner
            total[:, 2 * width :] = down
        else:
            total[:, : 2 * width] += inner
            total[:, 2 * width :] += down
    for block in range(half // 128):
        for column in range(4):
            for matrix in range(3):
                first = matrix * width + column * 128
                last = (column * 3 + matrix) * 128
                out_ref[block ^ s_ref[1], :, last : last + 128] = total[
                    block * 128 : (block + 1) * 128, first : first + 128
                ].astype(BF16)


def hidden_grads(rows, cots, both, hiddens, scalars):
    size, depth = rows[0].shape
    width = hiddens[0].shape[1]
    half = depth // 2
    out = (4, 128, 3 * width)
    return call(
        hidden_grad_kernel,
        "hidden_grads",
        shaped(out),
        [pl.BlockSpec(memory_space=pl.ANY)] * 24,
        (*rows, *cots, *both, *hiddens),
        out_specs=full(out),
        scalars=scalars,
        scratch=[
            pltpu.VMEM((half, 3 * width), F32),
            pltpu.VMEM((2, size, half), BF16),
            pltpu.VMEM((2, size, half), BF16),
            pltpu.VMEM((2, size, 2 * width), BF16),
            pltpu.VMEM((2, size, width), BF16),
            pltpu.SemaphoreType.DMA((2, 4)),
        ],
        work=cost(24 * size * depth * width, 20 * size * depth),
    )


def split_kernel(_, a_ref, b_ref, *targets):
    width = targets[0].shape[1]
    for k, target in enumerate(targets):
        block, column = k % 4, slice(k // 4 * width, (k // 4 + 1) * width)
        total = a_ref[block, :, column].astype(F32) + b_ref[block, :, column].astype(F32)
        target[...] = total.astype(BF16)


def split(left, right):
    _, rows, double = left.shape
    out = (rows, double // 2)
    return call(
        split_kernel,
        "split",
        [shaped(out)] * BLOCK,
        [full(left.shape), full(right.shape)],
        (left, right),
        out_specs=[full(out)] * BLOCK,
        work=cost(0, 6 * left.size),
    )


def add(*arrays):
    total = arrays[0].astype(F32)
    for array in arrays[1:]:
        total = total + array.astype(F32)
    return total.astype(BF16)


def after(value, *others):
    return lax.optimization_barrier((value, *others))[0]


def window_moves(rule):
    def target(d, t):
        core, place = rule[d & 1, t]
        return (d & ~1) | core, place

    return target


FIRST = window_moves(
    {
        (0, 0): (1, 0), (0, 1): (0, 0), (0, 2): (0, 1), (0, 3): (0, 2),
        (1, 0): (1, 1), (1, 1): (1, 2), (1, 2): (1, 3), (1, 3): (0, 3),
    }
)
SECOND = window_moves(
    {
        (0, 0): (1, 1), (0, 1): (0, 0), (0, 2): (0, 1), (0, 3): (0, 3),
        (1, 0): (1, 0), (1, 1): (1, 2), (1, 2): (1, 3), (1, 3): (0, 2),
    }
)
THIRD = window_moves(
    {
        (0, 0): (0, 1), (0, 1): (0, 0), (0, 2): (0, 2), (0, 3): (0, 3),
        (1, 0): (1, 0), (1, 1): (1, 1), (1, 2): (1, 3), (1, 3): (1, 2),
    }
)
SECOND_BACK = window_moves(
    {
        (0, 0): (0, 1), (0, 1): (0, 2), (0, 2): (1, 3), (0, 3): (0, 3),
        (1, 0): (1, 0), (1, 1): (0, 0), (1, 2): (1, 1), (1, 3): (1, 2),
    }
)
FIRST_BACK = window_moves(
    {
        (0, 0): (0, 1), (0, 1): (0, 2), (0, 2): (0, 3), (0, 3): (1, 3),
        (1, 0): (0, 0), (1, 1): (1, 0), (1, 2): (1, 1), (1, 3): (1, 2),
    }
)


def collect_window(links, own, tip, early, late):
    first = links.move(own, FIRST)
    second = links.move(after(jnp.where(tip, own, first), *early), SECOND)
    third = links.move(after(second, *late), THIRD)
    sources = []
    for array in (own, first, second, third):
        sources += [array, links.swap(array, CORE)]
    return sources + [sources[5], sources[4]], second, third


def return_window(links, parts, owned, line):
    got = [links.swap(part, CORE) for part in parts[::-1]][::-1]
    inside = (line == 1) | (line == 2)
    zero = jnp.zeros((), BF16)
    last = add(parts[3], got[3])
    third = links.move(last, THIRD)
    outer_end = inside & ~owned
    second = links.move(
        jnp.where(outer_end, last, add(parts[2], got[2], jnp.where(inside, third, zero))), SECOND_BACK
    )
    first = links.move(
        add(
            jnp.where(inside, second, zero),
            jnp.where(owned, parts[1], zero),
            jnp.where(owned, got[1], zero),
        ),
        FIRST_BACK,
    )
    return first, second, parts[0], got[0]


def collect_block(links, rows):
    half = rows.shape[0] // 2
    side, near = links.swap(rows, SIDE), links.swap(rows, NEAR)
    corner = jnp.concatenate(
        [links.swap(near[:half], SIDE), links.swap(side[half:], NEAR)], axis=0
    )
    return rows, side, near, corner


def collect_block_late(links, rows, gate):
    side = links.swap(rows, SIDE)
    near = links.swap(after(rows, gate), NEAR)
    return rows, side, near


def per_device(
    links,
    tokens,
    lengths,
    cotangent,
    attention_gain,
    attention_bias,
    query_weight,
    key_weight,
    value_weight,
    out_weight,
    feedforward_gain,
    feedforward_bias,
    gate_weight,
    up_weight,
    down_weight,
):
    outer = links.outer
    dp = lax.axis_index("dp")
    line = lax.axis_index("tensor")
    core, inner = dp % 2, dp % BLOCK
    side_bit, far_bit = dp // 2 % 2, dp // 4 % 2
    near_bit = line % 2
    window = line // 2
    owned = core == window
    ends = (line == 0) | (line == 3)
    share = near_bit * 2 + core
    hidden_share = near_bit * 4 + side_bit * 2 + core
    width = query_weight.shape[1]
    chunk, depth = tokens.shape

    def by_block(array):
        if outer == 1:
            return array
        shape = (array.shape[0], outer, BLOCK, depth // (outer * BLOCK))
        return array.reshape(shape).transpose(0, 2, 1, 3).reshape(array.shape)

    qkv = links.gather_outer(jnp.stack([query_weight, key_weight, value_weight]), 1)
    pair = jnp.stack(
        [
            links.move(
                qkv, lambda d, t, k=k: ((d & ~1) | (t % 2), t // 2 + 2 * ((d & 1) ^ k))
            )
            for k in range(2)
        ]
    )
    corner_mask = (SIDE[0] | FAR_SIDE[0], 0)
    quads = [pair] + [links.swap(pair, mask) for mask in (SIDE, FAR_SIDE, corner_mask)]

    order_chunk = jnp.arange(4, dtype=jnp.int32) ^ share
    positions = (order_chunk[:, None] * chunk + jnp.arange(chunk, dtype=jnp.int32)).reshape(-1)
    lane = jnp.arange(128, dtype=jnp.int32)
    frequency = jnp.power(ROTARY_BASE, -(lane % (HEAD // 2)).astype(F32) * 2.0 / HEAD)
    angles = positions.astype(F32)[:, None] * frequency[None, :]
    cosine = jnp.cos(angles)
    sine = jnp.sin(angles) * jnp.where(lane % HEAD < HEAD // 2, -1.0, 1.0)

    blocks = pack_hidden(
        links.gather_outer(gate_weight, 0),
        links.gather_outer(up_weight, 0),
        links.gather_outer(down_weight, 1),
        hidden_share,
    )
    mine = jnp.stack(
        [blocks[0]]
        + [
            links.swap(
                blocks[k],
                ((SIDE[0] if k & 2 else 0) | (k & 1), NEAR[1] if k & 4 else 0),
            )
            for k in range(1, BLOCK)
        ]
    )

    normed_first = norm_rows(tokens, attention_gain, attention_bias)
    sources, second_round, last_round = collect_window(
        links, normed_first, owned & ends, (pair, cosine, sine), (*quads, mine)
    )

    piece = after(links.gather_outer(out_weight.T, 0), second_round)
    both_mask = (0, NEAR[1] | FAR[1])
    line_pieces = jnp.stack([piece, links.swap(piece, NEAR)])
    line_pieces = jnp.concatenate([line_pieces, links.swap(line_pieces, FAR)])
    mine = after(mine, last_round)
    far, far_side = links.swap(mine, FAR), links.swap(mine, FAR_SIDE)
    length = jnp.where(core == window, lengths, links.swap(lengths, CORE))
    bias = jnp.where(positions < length[0], 0.0, MASKED).astype(F32)
    bias = jnp.broadcast_to(bias[:, None], (WIN, 128))
    slot = jnp.arange(4, dtype=jnp.int32)
    slot_chunk = jnp.where(line < 2, line + slot, line - slot) % 4
    last_source = jnp.where(ends, 1 - owned.astype(jnp.int32), 3 - owned.astype(jnp.int32))
    scalars = jnp.concatenate(
        [
            slot_chunk ^ share,
            jnp.stack([(inner // 2) * 2 + window, 1 - owned.astype(jnp.int32), last_source]),
        ]
    ).astype(jnp.int32)

    query, key, value, key_t, value_t, rows_first, weight_qkv = project(
        sources, quads, cosine, sine, scalars, outer
    )
    def to_owner(k):
        def rule(d, t):
            return (d & ~1) | (t // 2), ((t % 2) * 2 + (d & 1)) ^ k

        return rule

    pieces = after(line_pieces, query)
    out_own = jnp.stack([pieces, links.swap(pieces, SIDE)])
    m0, m1, lse = attend(after(query, mine), key, value_t, bias, chunk, 0)
    cots = collect_block_late(links, after(cotangent, last_round), mine)
    weight_in, weight_down = place_hidden(
        mine, far_side, far, links.swap(after(far, m0), FAR_SIDE), inner, outer
    )
    m2, m3, lse_late = attend(after(query, m0, far_side, far, out_own, cots[1]), key, value_t, bias, chunk, 1)
    mixed, lse = (m0, m1, m2, m3), jnp.concatenate([lse, lse_late], axis=2)

    def to_heads(k):
        def rule(d, t):
            who = t ^ k
            return (d & ~1) | (who & 1), (who >> 1) + 2 * (d & 1)

        return rule

    attended = [links.move(mixed[k], to_owner(k)) for k in range(2)]
    out_own = jnp.concatenate([out_own, links.swap(out_own, FAR_SIDE)])
    gates = (m2, *attended)
    attended += [links.move(after(mixed[k], *gates), to_owner(k)) for k in (2, 3)]
    out_other = links.swap(after(out_own, *gates), CORE)
    corner = links.swap(after(cots[2], *gates), SIDE)
    cots = [(part, links.swap(after(part, *gates), CORE)) for part in cots]
    residual, normed_second, weight_out = out_norm(
        attended, out_own, out_other, after(tokens, far, *cots[1], *cots[2]), feedforward_gain, feedforward_bias, inner, outer
    )

    masks = (SIDE, NEAR, (SIDE[0], NEAR[1]))
    fed, others, totals, gates = [], [], [], ()
    cots.append((corner, links.swap(after(corner, normed_second), CORE)))
    grad_hidden = [hidden_back(cot, weight_down) for cot in cots]
    rows = []
    for q, part in enumerate(collect_block(links, normed_second)):
        rows.append((part, links.swap(part, CORE)))
        own_rows = after(part, *gates)
        fed.append(feed((own_rows, rows[q][1]), grad_hidden[q], weight_in, weight_down))
        others.append(links.swap(fed[q][4], CORE))
        gates = (fed[q][0], *totals[-1:])
        if q:
            totals.append(add(fed[q][2], others[q][:, :depth]))
    back_sent = [links.swap(total, mask) for total, mask in zip(totals, masks, strict=True)]
    hiddens, boths, backs, outs, _ = zip(*fed, strict=True)

    def hidden_half(index, *gates):
        flat = [part for pair_rows in rows for part in pair_rows]
        flat[0] = after(flat[0], *gates)
        flat_cots = [part for cot in cots for part in cot]
        if outer > 1:
            flat = [by_block(part) for part in flat]
            flat_cots = [by_block(part) for part in flat_cots]
        where = jnp.stack([index, side_bit * 2 + core])
        return hidden_grads(flat, flat_cots, boths, hiddens, where)

    hidden_given = hidden_half(1 - far_bit, *totals)
    hidden_got = links.swap(hidden_given, FAR_SIDE)
    out_totals = [add(outs[q], others[q][:, depth:]) for q in (1, 3)]
    grad_residual, grad_attn, *grad_attended, sums_second = middle_back(
        (backs[0], others[0][:, :depth], *back_sent),
        after(cotangent, hidden_given, *out_totals),
        residual,
        feedforward_gain,
        weight_out,
    )
    grad_mixed = [links.move(grad_attended[k], to_heads(k)) for k in range(4)]

    hidden_kept = hidden_half(far_bit, grad_attn)
    out_sent = [links.swap(after(total, *grad_mixed), SIDE) for total in out_totals]
    out_total = add(outs[2], others[2][:, depth:], out_sent[1])
    out_sent[1] = links.swap(out_total, NEAR)
    layer_out = (
        residual
        + outs[0].astype(F32)
        + others[0][:, depth:].astype(F32)
        + out_sent[0].astype(F32)
        + out_sent[1].astype(F32)
    ).astype(BF16)

    sums = add(hidden_kept, hidden_got)
    half = sums.shape[2] // 2
    near_part, far_part = sums[:, :, :half], sums[:, :, half:]
    far_got = links.swap(far_part, FAR)
    grad_mixed[0] = after(grad_mixed[0], near_part)
    terms = (query, key, value, key_t, mixed, grad_mixed, lse, bias, cosine, sine)
    back_first = attend_back(0, *terms)
    parts = split(after(near_part, back_first[0]), far_got)
    back_second = attend_back(1, after(query, parts[0], out_sent[0], out_total), *terms[1:])
    parts = [parts[0]] + [
        links.swap(parts[k], ((SIDE[0] if k & 2 else 0) | (k & 1), NEAR[1] if k & 4 else 0))
        for k in range(1, BLOCK)
    ]
    parts = [links.scatter_outer(part, 0) for part in parts]
    gate_grad, up_grad, down_grad = deliver(parts, hidden_share)

    grads = [part for both in zip(back_first, back_second, strict=True) for part in both]
    weight_qkv = after(
        weight_qkv.reshape(depth, 3 * width), out_sent[1], *parts
    )
    sums = [None] * 4
    for slot in (3, 2, 1, 0):
        sums[slot] = unproject(grads, weight_qkv, scalars, slot)
    kept, given = out_grad_blocks(after(by_block(grad_attn), sums[2]), attended, inner)
    out_wide = add(kept, links.swap(given, CORE))
    out_first = add(
        out_wide[0], *(links.swap(out_wide[q], mask) for q, mask in ((1, SIDE), (2, FAR_SIDE), (3, corner_mask)))
    )
    out_sums = add(
        out_first[:, :width],
        *(
            links.swap(out_first[:, q * width : (q + 1) * width], mask)
            for q, mask in ((1, NEAR), (2, FAR), (3, both_mask))
        ),
    )
    out_grad = links.scatter_outer(out_sums, 0).astype(F32).T

    blocks = weight_grad(after(by_block(rows_first), sums[2]), grads, scalars)
    blocks = blocks.reshape(4, 2 * (depth // BLOCK), 3 * width)
    wide = add(
        blocks[0],
        *(links.swap(blocks[q], mask) for q, mask in ((1, SIDE), (2, FAR_SIDE), (3, corner_mask))),
    )
    rows_each = depth // BLOCK
    halves = [
        links.move(
            wide[k * rows_each : (k + 1) * rows_each],
            lambda d, t, k=k: ((d & ~1) | ((t // 2) ^ k), (t % 2) * 2 + (d & 1)),
        )
        for k in range(2)
    ]
    tokens_grad, sums_first = first_back(
        return_window(links, sums, owned, line),
        grad_residual,
        after(tokens, *halves, out_sums),
        attention_gain,
        jnp.stack([owned, owned & ends]),
    )

    sums = links.scatter_outer(add(*halves), 0).astype(F32)

    norms = jnp.concatenate([sums_first, sums_second], axis=0)
    side, far, corner = (links.swap(norms, mask) for mask in (SIDE, FAR_SIDE, corner_mask))
    norms = (norms + side) + (far + corner)
    near, far, both = (links.swap(norms, mask) for mask in (NEAR, FAR, both_mask))
    norms = (norms + near) + (far + both)
    norms = norms + links.swap(norms, CORE)
    for bit in range(3, links.nd.bit_length() - 1):
        norms = norms + links.swap(norms, (1 << bit, 0))
    return (
        layer_out,
        tokens_grad,
        norms[0],
        norms[1],
        sums[:, :width],
        sums[:, width : 2 * width],
        sums[:, 2 * width :],
        out_grad,
        norms[2],
        norms[3],
        gate_grad,
        up_grad,
        down_grad,
    )


def solution(mesh):
    rows, columns = P("dp", "tensor"), P("tensor", "dp")
    spread = P(("dp", "tensor"), None)
    placed = (
        spread, P("dp"), spread, P(), P(), rows, rows, rows, columns, P(), P(), rows, rows, columns
    )
    given = (
        spread, spread, P(), P(), rows, rows, rows, columns, P(), P(), rows, rows, columns
    )
    return jax.shard_map(
        functools.partial(per_device, Links(mesh)),
        mesh=mesh,
        in_specs=placed,
        out_specs=given,
        check_vma=False,
    )
```
